128 devices in a mesh: samp: 4 (over z_hi, core), pair: 32 (over y, x, z_lo).
Axes of the slice: x: 4, y: 4, z: 4 (z_hi: 2, z_lo: 2; z = z_hi * 2 + z_lo), core: 2. Of those that a mesh axis runs over, the one named last changes fastest.
Arguments:
- matrix: bfloat16 [32768, 16384], P('samp', 'pair'), may hold values from -48 to 48
- tournament: int32 [2, 32], replicated, may hold values from 0 to 1
Outputs:
- result: bfloat16 [32768, 16384], P('samp', 'pair')
The draws below stay inside these ranges and needn't reach their ends.
All inputs are finite; a program needn't handle non-finite values.
Results may differ from the reference program's by a relative error of at most 0.008.
Values may be sent and summed in bfloat16 or wider, within the bound.
A program may use at most 128 MiB of HBM per device.

```python
import math
import jax
import jax.numpy as jnp
from jax import lax

BLOCK_COLS = 256
ROUNDS = 2
POLAR_STEPS = 5
SAMPLES = 32768
COLUMNS = 16384


def draw_matrix(key, part):
    sample_pos = jnp.arange(SAMPLES, dtype=jnp.float32)
    sample_ramp = jnp.exp(0.55 * sample_pos / SAMPLES)
    jitter = jnp.exp(jax.random.uniform(jax.random.fold_in(key, 1), (SAMPLES,), jnp.float32, math.log(0.5), math.log(3.0)))
    column_scale = jnp.exp(jax.random.uniform(jax.random.fold_in(key, 2), (COLUMNS,), jnp.float32, math.log(0.4), math.log(4.0)))
    base_values = jnp.clip(jax.random.normal(jax.random.fold_in(key, 3), (SAMPLES, COLUMNS), jnp.float32), -4.0, 4.0)
    return (0.5 * base_values * (sample_ramp * jitter)[:, None] * column_scale[None, :]).astype(jnp.bfloat16)


def place_ends(array, own_key, least, top_value):
    longest = array.shape.index(max(array.shape))
    spots = []
    for shift in (0, 1):
        where = [jax.random.randint(jax.random.fold_in(own_key, axis), (), 0, length) for axis, length in enumerate(array.shape)]
        where[longest] = (where[longest] + shift) % array.shape[longest]
        spots.append(tuple(where))
    return array.at[spots[0]].set(least).at[spots[1]].set(top_value)


def setup_inputs(seed: int = 0) -> dict:
    splits = jax.random.split(jax.random.key(seed), 3)
    matrix = draw_matrix(jax.random.fold_in(splits[2], 71), 0)
    tournament = place_ends(jax.random.randint(splits[1], (ROUNDS, COLUMNS // (2 * BLOCK_COLS)), 0, 2), jax.random.fold_in(splits[1], 1), 0, 1).astype(jnp.int32)
    return dict(matrix=matrix, tournament=tournament)


coupling = 2.0
start_scale = 6.0

def polar_rotation(cross_gram):
    block_width = cross_gram.shape[0]
    frobenius = jnp.sqrt(jnp.sum(cross_gram * cross_gram) + 1e-06)
    coupled = coupling * cross_gram / frobenius
    blank_block = jnp.zeros_like(coupled)
    skew_matrix = jnp.concatenate([jnp.concatenate([blank_block, -coupled], 1), jnp.concatenate([coupled.T, blank_block], 1)], 0)
    iterate = (jnp.eye(2 * block_width, dtype=coupled.dtype) + skew_matrix) / start_scale
    for iteration in range(POLAR_STEPS):
        rounded = iterate.astype(jnp.bfloat16)
        square = lax.dot_general(rounded, rounded, (((0,), (0,)), ((), ())), preferred_element_type=jnp.float32).astype(jnp.bfloat16)
        iterate = 1.5 * iterate - 0.5 * jnp.dot(rounded, square, preferred_element_type=jnp.float32)
    return iterate.astype(jnp.bfloat16)

def slot_round(inputs):
    current, selector = inputs
    block_width = current.shape[1] // 2
    cross_gram = lax.dot_general(current[:, :block_width], current[:, block_width:], (((0,), (0,)), ((), ())), preferred_element_type=jnp.float32)
    rotation = polar_rotation(cross_gram)
    rotated = jnp.dot(current, rotation, preferred_element_type=jnp.float32).astype(jnp.bfloat16)
    first_half = rotated[:, :block_width]
    second_half = rotated[:, block_width:]
    kept_block = jnp.where(selector == 1, second_half, first_half)
    moving_block = jnp.where(selector == 1, first_half, second_half)
    return (kept_block, moving_block)

def reference(matrix, tournament):
    slot_count = COLUMNS // (2 * BLOCK_COLS)
    blocks = matrix.reshape(SAMPLES, slot_count, 2 * BLOCK_COLS).transpose(1, 0, 2)
    for tourney in range(ROUNDS):
        kept_block, moving_block = lax.map(slot_round, (blocks, tournament[tourney]))
        blocks = jnp.concatenate([jnp.roll(kept_block, -(slot_count // 2), axis=0), jnp.roll(moving_block, 1, axis=0)], axis=2)
    return blocks.transpose(1, 0, 2).reshape(SAMPLES, COLUMNS)
```

```python
import functools

import jax
import jax.numpy as jnp
from jax import lax
from jax.experimental import pallas as pl
from jax.experimental.pallas import tpu as pltpu
from jax.sharding import PartitionSpec as P

POLAR_STEPS = 5
MESH = pl.DeviceIdType.MESH
COUPLING = 2.0
START_SCALE = 6.0
CHUNKS = 8
TILES = 2
F32 = jnp.float32
BF16 = jnp.bfloat16


def over_rows(a, b):
    return lax.dot_general(a, b, (((0,), (0,)), ((), ())), preferred_element_type=F32)


def mul(a, b):
    return jnp.dot(a, b, preferred_element_type=F32)


def half_rows(upper, lower):
    rows = jnp.concatenate([upper, lower], 1) / START_SCALE
    for _ in range(POLAR_STEPS):
        rounded = rows.astype(BF16)
        square = lax.dot_general(
            rounded, rounded, (((1,), (1,)), ((), ())), preferred_element_type=F32
        ).astype(BF16)
        rows = 1.5 * rows - 0.5 * mul(square, rounded)
    return rows.astype(BF16)


def rotation_into(gram, chosen, keep_ref, move_ref):
    width = gram.shape[0]
    coupled = COUPLING * gram / jnp.sqrt(jnp.sum(gram * gram) + 1e-06)
    row = lax.broadcasted_iota(jnp.int32, (width, width), 0)
    eye = (row == lax.broadcasted_iota(jnp.int32, (width, width), 1)).astype(F32)
    top = half_rows(eye, -coupled)
    bottom = half_rows(coupled.T, eye)
    last = chosen == 1
    for i, part in enumerate((top, bottom)):
        first_cols, second_cols = part[:, :width].astype(F32), part[:, width:].astype(F32)
        rows = pl.ds(i * width, width)
        keep_ref[rows, :] = jnp.where(last, second_cols, first_cols).astype(BF16)
        move_ref[rows, :] = jnp.where(last, first_cols, second_cols).astype(BF16)


def kernel(
    tour_ref, y_hbm, out_ref,
    y_ref, kept, moving, arrived, moved, keep_cols, move_cols, acc, wide_in, narrow_out, narrow_in,
    load_sem, send_sem, recv_sem, ex_send, ex_recv,
):
    samp, pair = lax.axis_index("samp"), lax.axis_index("pair")
    slots = lax.axis_size("pair")
    half = slots // 2
    ahead = lax.rem(pair + half + 1, slots)
    behind = lax.rem(pair + half - 1, slots)
    core_peer = samp + 1 - 2 * lax.rem(samp, 2)
    far_peer = lax.rem(samp + 2, 4)
    height, width = kept.shape
    chunk = height // CHUNKS
    tile = chunk // TILES

    loads = [
        pltpu.make_async_copy(
            y_hbm.at[pl.ds(i * chunk, chunk)], y_ref.at[pl.ds(i * chunk, chunk)], load_sem.at[i]
        )
        for i in range(CHUNKS)
    ]
    for load in loads:
        load.start()
    barrier = pltpu.get_barrier_semaphore()
    for where in ({"pair": ahead}, {"pair": behind}, {"samp": core_peer}, {"samp": far_peer}):
        pl.semaphore_signal(barrier, inc=1, device_id=where, device_id_type=MESH)

    def add_gram(a_ref, b_ref, a_cols, b_cols, i):
        def body(t, carry):
            rows = pl.ds(pl.multiple_of(i * chunk + t * tile, tile), tile)
            acc[...] += over_rows(a_ref[rows, a_cols], b_ref[rows, b_cols])
            return carry

        lax.fori_loop(0, TILES, body, 0)

    def summed_gram(step):
        near = pltpu.make_async_remote_copy(
            acc, wide_in.at[step], ex_send.at[2 * step], ex_recv.at[2 * step],
            device_id={"samp": core_peer}, device_id_type=MESH,
        )
        near.start()
        near.wait()
        chip = (acc[...] + wide_in[step]).astype(BF16)
        narrow_out[step] = chip
        far = pltpu.make_async_remote_copy(
            narrow_out.at[step], narrow_in.at[step], ex_send.at[2 * step + 1], ex_recv.at[2 * step + 1],
            device_id={"samp": far_peer}, device_id_type=MESH,
        )
        far.start()
        far.wait()
        return chip.astype(F32) + narrow_in[step].astype(F32)

    def hop(source, target, i, step):
        return pltpu.make_async_remote_copy(
            source, target, send_sem.at[step, i], recv_sem.at[step, i],
            device_id={"pair": ahead}, device_id_type=MESH,
        )

    low, high = pl.ds(0, width), pl.ds(width, width)
    acc[...] = jnp.zeros_like(acc)
    for i in range(CHUNKS):
        loads[i].wait()
        add_gram(y_ref, y_ref, low, high, i)
    pl.semaphore_wait(barrier, 4)
    rotation_into(summed_gram(0), tour_ref[0, pair], keep_cols, move_cols)

    def first_move(i):
        rows = pl.ds(pl.multiple_of(i * chunk, chunk), chunk)
        return hop(moving.at[rows], arrived.at[rows], i, 0)

    def second_move(i):
        rows = pl.ds(pl.multiple_of(i * chunk, chunk), chunk)
        return hop(moved.at[rows], out_ref.at[rows, high], i, 1)

    def rotate_first(cols_ref, to_ref, i):
        def body(t, carry):
            rows = pl.ds(pl.multiple_of(i * chunk + t * tile, tile), tile)
            to_ref[rows, :] = mul(y_ref[rows, :], cols_ref[...]).astype(BF16)
            return carry

        lax.fori_loop(0, TILES, body, 0)

    def rotate_second(cols_ref, to_ref, i):
        def body(t, carry):
            rows = pl.ds(pl.multiple_of(i * chunk + t * tile, tile), tile)
            total = mul(kept[rows, :], cols_ref[low, :]) + mul(arrived[rows, :], cols_ref[high, :])
            to_ref[rows, low] = total.astype(BF16)
            return carry

        lax.fori_loop(0, TILES, body, 0)

    @pl.loop(0, CHUNKS)
    def _(i):
        rotate_first(move_cols, moving, i)
        first_move(i).start()

    @pl.loop(0, CHUNKS)
    def _(i):
        rotate_first(keep_cols, kept, i)

    acc[...] = jnp.zeros_like(acc)

    @pl.loop(0, CHUNKS)
    def _(i):
        first_move(i).wait_recv()
        add_gram(kept, arrived, low, low, i)

    rotation_into(summed_gram(1), tour_ref[1, lax.rem(pair + half, slots)], keep_cols, move_cols)

    @pl.loop(0, CHUNKS)
    def _(i):
        rotate_second(move_cols, moved, i)
        second_move(i).start()

    @pl.loop(0, CHUNKS)
    def _(i):
        rotate_second(keep_cols, out_ref, i)

    @pl.loop(0, CHUNKS)
    def _(i):
        first_move(i).wait_send()
        second_move(i).wait()


def shards(matrix, tournament):
    height, columns = matrix.shape
    width = columns // 2
    block = pltpu.VMEM((height, width), BF16)
    return pl.pallas_call(
        kernel,
        out_shape=jax.ShapeDtypeStruct((height, columns), BF16),
        in_specs=[pl.BlockSpec(memory_space=pltpu.SMEM), pl.BlockSpec(memory_space=pl.ANY)],
        out_specs=pl.BlockSpec(memory_space=pltpu.VMEM),
        scratch_shapes=[
            pltpu.VMEM((height, columns), BF16), block, block, block, block,
            pltpu.VMEM((columns, width), BF16), pltpu.VMEM((columns, width), BF16),
            pltpu.VMEM((width, width), F32), pltpu.VMEM((2, width, width), F32),
            pltpu.VMEM((2, width, width), BF16), pltpu.VMEM((2, width, width), BF16),
            pltpu.SemaphoreType.DMA((CHUNKS,)),
            pltpu.SemaphoreType.DMA((2, CHUNKS)), pltpu.SemaphoreType.DMA((2, CHUNKS)),
            pltpu.SemaphoreType.DMA((4,)), pltpu.SemaphoreType.DMA((4,)),
        ],
        compiler_params=pltpu.CompilerParams(
            collective_id=0, has_side_effects=True, vmem_limit_bytes=56 * 1024 * 1024
        ),
    )(tournament, matrix)


def solution(mesh):
    placed = (P("samp", "pair"), P())
    return jax.shard_map(
        shards, mesh=mesh, in_specs=placed, out_specs=P("samp", "pair"), check_vma=False
    )
```

```python
import functools

import jax
import jax.numpy as jnp
from jax import lax
from jax.experimental import pallas as pl
from jax.experimental.pallas import tpu as pltpu
from jax.sharding import PartitionSpec as P

POLAR_STEPS = 5
MESH = pl.DeviceIdType.MESH
COUPLING = 2.0
START_SCALE = 6.0
CHUNKS = 8
TILES = 2
F32 = jnp.float32
BF16 = jnp.bfloat16


def over_rows(a, b):
    return lax.dot_general(a, b, (((0,), (0,)), ((), ())), preferred_element_type=F32)


def mul(a, b):
    return jnp.dot(a, b, preferred_element_type=F32)


def half_rows(upper, lower):
    rows = jnp.concatenate([upper, lower], 1) / START_SCALE
    for _ in range(POLAR_STEPS):
        rounded = rows.astype(BF16)
        square = lax.dot_general(
            rounded, rounded, (((1,), (1,)), ((), ())), preferred_element_type=F32
        ).astype(BF16)
        rows = 1.5 * rows - 0.5 * mul(square, rounded)
    return rows.astype(BF16)


def rotation_into(gram, chosen, keep_ref, move_ref):
    width = gram.shape[0]
    coupled = COUPLING * gram / jnp.sqrt(jnp.sum(gram * gram) + 1e-06)
    row = lax.broadcasted_iota(jnp.int32, (width, width), 0)
    eye = (row == lax.broadcasted_iota(jnp.int32, (width, width), 1)).astype(F32)
    top = half_rows(eye, -coupled)
    bottom = half_rows(coupled.T, eye)
    last = chosen == 1
    for i, part in enumerate((top, bottom)):
        first_cols, second_cols = part[:, :width].astype(F32), part[:, width:].astype(F32)
        rows = pl.ds(i * width, width)
        keep_ref[rows, :] = jnp.where(last, second_cols, first_cols).astype(BF16)
        move_ref[rows, :] = jnp.where(last, first_cols, second_cols).astype(BF16)


def kernel(
    tour_ref, y_hbm, out_ref,
    y_ref, kept, moving, arrived, moved, keep_cols, move_cols, acc, wide_in, narrow_out, narrow_in,
    load_sem, send_sem, recv_sem, ex_send, ex_recv,
):
    samp, pair = lax.axis_index("samp"), lax.axis_index("pair")
    slots = lax.axis_size("pair")
    half = slots // 2
    ahead = lax.rem(pair + half + 1, slots)
    behind = lax.rem(pair + half - 1, slots)
    core_peer = samp + 1 - 2 * lax.rem(samp, 2)
    far_peer = lax.rem(samp + 2, 4)
    height, width = kept.shape
    chunk = height // CHUNKS
    tile = chunk // TILES

    loads = [
        pltpu.make_async_copy(
            y_hbm.at[pl.ds(i * chunk, chunk)], y_ref.at[pl.ds(i * chunk, chunk)], load_sem.at[i]
        )
        for i in range(CHUNKS)
    ]
    for load in loads:
        load.start()
    barrier = pltpu.get_barrier_semaphore()
    for where in ({"pair": ahead}, {"pair": behind}, {"samp": core_peer}, {"samp": far_peer}):
        pl.semaphore_signal(barrier, inc=1, device_id=where, device_id_type=MESH)

    def add_gram(a_ref, b_ref, a_cols, b_cols, i):
        def body(t, carry):
            rows = pl.ds(pl.multiple_of(i * chunk + t * tile, tile), tile)
            acc[...] += over_rows(a_ref[rows, a_cols], b_ref[rows, b_cols])
            return carry

        lax.fori_loop(0, TILES, body, 0)

    def summed_gram(step):
        near = pltpu.make_async_remote_copy(
            acc, wide_in.at[step], ex_send.at[2 * step], ex_recv.at[2 * step],
            device_id={"samp": core_peer}, device_id_type=MESH,
        )
        near.start()
        near.wait()
        chip = (acc[...] + wide_in[step]).astype(BF16)
        narrow_out[step] = chip
        far = pltpu.make_async_remote_copy(
            narrow_out.at[step], narrow_in.at[step], ex_send.at[2 * step + 1], ex_recv.at[2 * step + 1],
            device_id={"samp": far_peer}, device_id_type=MESH,
        )
        far.start()
        far.wait()
        return chip.astype(F32) + narrow_in[step].astype(F32)

    def hop(source, target, i, step):
        return pltpu.make_async_remote_copy(
            source, target, send_sem.at[step, i], recv_sem.at[step, i],
            device_id={"pair": ahead}, device_id_type=MESH,
        )

    low, high = pl.ds(0, width), pl.ds(width, width)
    acc[...] = jnp.zeros_like(acc)
    for i in range(CHUNKS):
        loads[i].wait()
        add_gram(y_ref, y_ref, low, high, i)
    pl.semaphore_wait(barrier, 4)
    rotation_into(summed_gram(0), tour_ref[0, pair], keep_cols, move_cols)

    def first_move(i):
        rows = pl.ds(pl.multiple_of(i * chunk, chunk), chunk)
        return hop(moving.at[rows], arrived.at[rows], i, 0)

    def second_move(i):
        rows = pl.ds(pl.multiple_of(i * chunk, chunk), chunk)
        return hop(moved.at[rows], out_ref.at[rows, high], i, 1)

    def rotate_first(cols_ref, to_ref, i):
        def body(t, carry):
            rows = pl.ds(pl.multiple_of(i * chunk + t * tile, tile), tile)
            to_ref[rows, :] = mul(y_ref[rows, :], cols_ref[...]).astype(BF16)
            return carry

        lax.fori_loop(0, TILES, body, 0)

    def rotate_second(cols_ref, to_ref, i):
        def body(t, carry):
            rows = pl.ds(pl.multiple_of(i * chunk + t * tile, tile), tile)
            total = mul(kept[rows, :], cols_ref[low, :]) + mul(arrived[rows, :], cols_ref[high, :])
            to_ref[rows, low] = total.astype(BF16)
            return carry

        lax.fori_loop(0, TILES, body, 0)

    @pl.loop(0, CHUNKS)
    def _(i):
        rotate_first(move_cols, moving, i)
        first_move(i).start()

    @pl.loop(0, CHUNKS)
    def _(i):
        rotate_first(keep_cols, kept, i)

    acc[...] = jnp.zeros_like(acc)

    @pl.loop(0, CHUNKS)
    def _(i):
        first_move(i).wait_recv()
        add_gram(kept, arrived, low, low, i)

    rotation_into(summed_gram(1), tour_ref[1, lax.rem(pair + half, slots)], keep_cols, move_cols)

    @pl.loop(0, CHUNKS)
    def _(i):
        rotate_second(move_cols, moved, i)
        second_move(i).start()

    @pl.loop(0, CHUNKS)
    def _(i):
        rotate_second(keep_cols, out_ref, i)

    @pl.loop(0, CHUNKS)
    def _(i):
        first_move(i).wait_send()
        second_move(i).wait()


def shards(matrix, tournament):
    height, columns = matrix.shape
    width = columns // 2
    block = pltpu.VMEM((height, width), BF16)
    return pl.pallas_call(
        kernel,
        out_shape=pltpu.VMEM((height, columns), BF16),
        in_specs=[pl.BlockSpec(memory_space=pltpu.SMEM), pl.BlockSpec(memory_space=pl.ANY)],
        out_specs=pl.BlockSpec(memory_space=pltpu.VMEM),
        scratch_shapes=[
            pltpu.VMEM((height, columns), BF16), block, block, block, block,
            pltpu.VMEM((columns, width), BF16), pltpu.VMEM((columns, width), BF16),
            pltpu.VMEM((width, width), F32), pltpu.VMEM((2, width, width), F32),
            pltpu.VMEM((2, width, width), BF16), pltpu.VMEM((2, width, width), BF16),
            pltpu.SemaphoreType.DMA((CHUNKS,)),
            pltpu.SemaphoreType.DMA((2, CHUNKS)), pltpu.SemaphoreType.DMA((2, CHUNKS)),
            pltpu.SemaphoreType.DMA((4,)), pltpu.SemaphoreType.DMA((4,)),
        ],
        compiler_params=pltpu.CompilerParams(
            collective_id=0, has_side_effects=True, vmem_limit_bytes=40 * 1024 * 1024
        ),
    )(tournament, matrix)


def solution(mesh):
    placed = (P("samp", "pair"), P())
    return jax.shard_map(
        shards, mesh=mesh, in_specs=placed, out_specs=P("samp", "pair"), check_vma=False
    )
```

```python
import jax
import jax.numpy as jnp
from jax import lax
from jax.experimental import pallas as pl
from jax.experimental.pallas import tpu as pltpu
from jax.sharding import PartitionSpec as P

POLAR_STEPS = 5
MESH = pl.DeviceIdType.MESH
COUPLING = 2.0
START_SCALE = 6.0
CHUNK = 128
TILE = 512
EARLY = 256
PIECES = ((0, 128), (128, 128))
F32 = jnp.float32
BF16 = jnp.bfloat16


def over_rows(a, b):
    return lax.dot_general(a, b, (((0,), (0,)), ((), ())), preferred_element_type=F32)


def mul(a, b):
    return jnp.dot(a, b, preferred_element_type=F32)


def rotation_into(gram, chosen, keep_ref, move_ref):
    width = gram.shape[0]
    coupled = COUPLING * gram / jnp.sqrt(jnp.sum(gram * gram) + 1e-06)
    row = lax.broadcasted_iota(jnp.int32, (width, width), 0)
    eye = (row == lax.broadcasted_iota(jnp.int32, (width, width), 1)).astype(F32)
    halves = [jnp.concatenate([eye, -coupled], 1) / START_SCALE, jnp.concatenate([coupled.T, eye], 1) / START_SCALE]
    for _ in range(POLAR_STEPS):
        rounded = [h.astype(BF16) for h in halves]
        squares = [lax.dot_general(r, r, (((1,), (1,)), ((), ())), preferred_element_type=F32) for r in rounded]
        squares = [(-0.5 * q).astype(BF16) for q in squares]
        halves = [1.5 * h + mul(q, r) for h, q, r in zip(halves, squares, rounded)]
    last = chosen == 1
    for i, h in enumerate(halves):
        first_cols, second_cols = h[:, :width], h[:, width:]
        rows = pl.ds(i * width, width)
        keep_ref[rows, :] = jnp.where(last, second_cols, first_cols).astype(BF16)
        move_ref[rows, :] = jnp.where(last, first_cols, second_cols).astype(BF16)


def kernel(
    tour_hbm, y_hbm, out_ref,
    tour_ref, tour_sem,
    y_ref, kept, moving, arrived, moved, early_in, early_kept, side_in,
    keep_cols, move_cols, far_keep, far_move, acc, wide_in, narrow_out, narrow_in, gram_out, gram_in,
    load_sem, send_sem, recv_sem, ex_send, ex_recv, early_send, early_recv, side_send, side_recv,
):
    samp, pair = lax.axis_index("samp"), lax.axis_index("pair")
    slots = lax.axis_size("pair")
    half = slots // 2

    def slot(by):
        return lax.rem(pair + (by + slots), slots)

    ahead = {"pair": slot(half + 1)}
    side = {"pair": slot(2)}
    core_peer = {"samp": samp + 1 - 2 * lax.rem(samp, 2)}
    far_peer = {"samp": lax.rem(samp + 2, 4)}
    height, width = kept.shape
    low, high = pl.ds(0, width), pl.ds(width, width)
    early = pl.ds(0, EARLY)
    n_early, n_chunks = EARLY // CHUNK, height // CHUNK

    def rows_of(i, size=CHUNK):
        return pl.ds(pl.multiple_of(i * size, size), size)

    def remote(source, target, send, recv, where):
        return pltpu.make_async_remote_copy(
            source, target, send, recv, device_id=where, device_id_type=MESH
        )

    n_loads = load_sem.shape[0]
    part = height // n_loads
    loads = [
        pltpu.make_async_copy(y_hbm.at[pl.ds(i * part, part)], y_ref.at[pl.ds(i * part, part)], load_sem.at[i])
        for i in range(n_loads)
    ]
    for load in loads:
        load.start()
    tour_load = pltpu.make_async_copy(tour_hbm, tour_ref, tour_sem)
    tour_load.start()
    barrier = pltpu.get_barrier_semaphore()
    greeted = (ahead, {"pair": slot(-half - 1)}, side, {"pair": slot(-2)}, core_peer, far_peer)
    for where in greeted:
        pl.semaphore_signal(barrier, inc=1, device_id=where, device_id_type=MESH)

    def summed_gram(step):
        near = remote(acc, wide_in.at[step], ex_send.at[4 * step], ex_recv.at[4 * step], core_peer)
        near.start()
        with jax.named_scope("near"):
            near.wait()
        chip = (acc[...] + wide_in[step]).astype(BF16)
        narrow_out[step] = chip
        far = remote(
            narrow_out.at[step], narrow_in.at[step], ex_send.at[4 * step + 1], ex_recv.at[4 * step + 1], far_peer
        )
        far.start()
        with jax.named_scope("far"):
            far.wait()
        total = (chip.astype(F32) + narrow_in[step].astype(F32)).astype(BF16)
        gram_out[step] = total
        passed_gram(step).start()
        if step == 0:
            early_move(1).start()
        return total.astype(F32)

    core = lax.rem(samp, 2)
    my_part = pl.ds(pl.multiple_of(core * (width // 2), width // 2), width // 2)

    def passed_gram(step):
        source, target = gram_out.at[step, my_part], gram_in.at[step, my_part]
        return remote(source, target, ex_send.at[4 * step + 2], ex_recv.at[4 * step + 2], ahead)

    def gram_from_behind(step):
        passed_gram(step).wait()
        half_gram = gram_in.at[step, my_part]
        share = remote(half_gram, half_gram, ex_send.at[4 * step + 3], ex_recv.at[4 * step + 3], core_peer)
        share.start()
        share.wait()
        return gram_in[step].astype(F32)

    def early_move(k):
        rows = pl.ds(*PIECES[k])
        return remote(y_hbm.at[rows], early_in.at[rows], early_send.at[k], early_recv.at[k], ahead)

    side_move = remote(moving.at[early], side_in, side_send, side_recv, side)

    def first_move(i):
        return remote(moving.at[rows_of(i)], arrived.at[rows_of(i)], send_sem.at[0, i], recv_sem.at[0, i], ahead)

    def second_move(i):
        return remote(
            moved.at[rows_of(i)], out_ref.at[rows_of(i), high], send_sem.at[1, i], recv_sem.at[1, i], ahead
        )

    def rotate_first(from_ref, cols_ref, to_ref, rows):
        to_ref[rows, :] = mul(from_ref[rows, :], cols_ref[...]).astype(BF16)

    def rotate_second(kept_ref, moved_ref, cols_ref, to_ref, to_cols, rows):
        total = mul(kept_ref[rows, :], cols_ref[low, :]) + mul(moved_ref[rows, :], cols_ref[high, :])
        to_ref[rows, to_cols] = total.astype(BF16)

    with jax.named_scope("gram0"):
        acc[...] = jnp.zeros_like(acc)
        for i in range(n_loads):
            loads[i].wait()
            rows = pl.ds(i * part, part)
            acc[...] += over_rows(y_ref[rows, low], y_ref[rows, high])
            if i == 0:
                tour_load.wait()
                pl.semaphore_wait(barrier, len(greeted))
                early_move(0).start()

    with jax.named_scope("exch0"):
        gram = summed_gram(0)
    with jax.named_scope("polar0"):
        rotation_into(gram, tour_ref[0, pair], keep_cols, move_cols)
    with jax.named_scope("moves0"):

        @pl.loop(n_early, n_chunks)
        def _(i):
            rotate_first(y_ref, move_cols, moving, rows_of(i))
            first_move(i).start()

        rotate_first(y_ref, move_cols, moving, early)

        @pl.loop(0, height // TILE)
        def _(i):
            rotate_first(y_ref, keep_cols, kept, rows_of(i, TILE))

    with jax.named_scope("gwait0"):
        gram = gram_from_behind(0)
    with jax.named_scope("farpolar0"):
        rotation_into(gram, tour_ref[0, slot(-half - 1)], far_keep, far_move)
    with jax.named_scope("early"):
        for k in range(len(PIECES)):
            early_move(k).wait()
        rotate_first(early_in, far_keep, early_kept, early)
        rotate_first(early_in, far_move, arrived, early)
        acc[...] = over_rows(kept[early, :], arrived[early, :])

    with jax.named_scope("gram1"):

        @pl.loop(n_early, n_chunks)
        def _(i):
            first_move(i).wait_recv()
            acc[...] += over_rows(kept[rows_of(i), :], arrived[rows_of(i), :])

    with jax.named_scope("exch1"):
        side_move.start()
        gram = summed_gram(1)
    with jax.named_scope("polar1"):
        rotation_into(gram, tour_ref[1, slot(half)], keep_cols, move_cols)
    with jax.named_scope("moves1"):

        @pl.loop(n_early, n_chunks)
        def _(i):
            rotate_second(kept, arrived, move_cols, moved, low, rows_of(i))
            second_move(i).start()

        @pl.loop(0, height // TILE)
        def _(i):
            rotate_second(kept, arrived, keep_cols, out_ref, low, rows_of(i, TILE))

    with jax.named_scope("gwait1"):
        gram = gram_from_behind(1)
    with jax.named_scope("farpolar1"):
        rotation_into(gram, tour_ref[1, slot(-1)], far_keep, far_move)
    with jax.named_scope("side"):
        side_move.wait()
        rotate_second(early_kept, side_in, far_move, out_ref, high, early)

    with jax.named_scope("last"):

        @pl.loop(n_early, n_chunks)
        def _(i):
            first_move(i).wait_send()
            second_move(i).wait()


def shards(matrix, tournament):
    height, columns = matrix.shape
    width = columns // 2
    block = pltpu.VMEM((height, width), BF16)
    short = pltpu.VMEM((EARLY, width), BF16)
    cols = pltpu.VMEM((columns, width), BF16)
    grams = pltpu.VMEM((2, width, width), BF16)
    copies = pltpu.SemaphoreType.DMA((2, height // CHUNK))
    one = pltpu.SemaphoreType.DMA
    return pl.pallas_call(
        kernel,
        out_shape=pltpu.VMEM((height, columns), BF16),
        in_specs=[pl.BlockSpec(memory_space=pl.ANY), pl.BlockSpec(memory_space=pl.ANY)],
        out_specs=pl.BlockSpec(memory_space=pltpu.VMEM),
        scratch_shapes=[
            pltpu.SMEM(tournament.shape, jnp.int32), pltpu.SemaphoreType.DMA,
            pltpu.VMEM((height, columns), BF16), block, block, block, block,
            pltpu.VMEM((EARLY, columns), BF16), short, short, cols, cols, cols, cols,
            pltpu.VMEM((width, width), F32), pltpu.VMEM((2, width, width), F32), grams, grams, grams, grams,
            pltpu.SemaphoreType.DMA((4,)), copies, copies,
            pltpu.SemaphoreType.DMA((8,)), pltpu.SemaphoreType.DMA((8,)),
            one((len(PIECES),)), one((len(PIECES),)), one, one,
        ],
        compiler_params=pltpu.CompilerParams(
            collective_id=0, has_side_effects=True, vmem_limit_bytes=40 * 1024 * 1024
        ),
    )(tournament, matrix)


def solution(mesh):
    placed = (P("samp", "pair"), P())
    return jax.shard_map(
        shards, mesh=mesh, in_specs=placed, out_specs=P("samp", "pair"), check_vma=False
    )
```

```python
import jax
import jax.numpy as jnp
from jax import lax
from jax.experimental import pallas as pl
from jax.experimental.pallas import tpu as pltpu
from jax.sharding import PartitionSpec as P

POLAR_STEPS = 5
MESH = pl.DeviceIdType.MESH
COUPLING = 2.0
START_SCALE = 6.0
CHUNK = 128
TILE = 512
EARLY = 256
PIECES = ((0, 128), (128, 128))
F32 = jnp.float32
BF16 = jnp.bfloat16


def over_rows(a, b):
    return lax.dot_general(a, b, (((0,), (0,)), ((), ())), preferred_element_type=F32)


def mul(a, b):
    return jnp.dot(a, b, preferred_element_type=F32)


def rotation_into(gram_ref, chosen, keep_ref, move_ref):
    gram = gram_ref[...].astype(F32)
    width = gram.shape[0]
    coupled = COUPLING * gram / jnp.sqrt(jnp.sum(gram * gram) + 1e-06)
    row = lax.broadcasted_iota(jnp.int32, (width, width), 0)
    eye = (row == lax.broadcasted_iota(jnp.int32, (width, width), 1)).astype(F32)
    halves = [jnp.concatenate([eye, -coupled], 1) / START_SCALE, jnp.concatenate([coupled.T, eye], 1) / START_SCALE]
    for _ in range(POLAR_STEPS):
        rounded = [h.astype(BF16) for h in halves]
        squares = [lax.dot_general(r, r, (((1,), (1,)), ((), ())), preferred_element_type=F32) for r in rounded]
        squares = [(-0.5 * q).astype(BF16) for q in squares]
        halves = [1.5 * h + mul(q, r) for h, q, r in zip(halves, squares, rounded)]
    last = chosen == 1
    for i, h in enumerate(halves):
        first_cols, second_cols = h[:, :width], h[:, width:]
        rows = pl.ds(i * width, width)
        keep_ref[rows, :] = jnp.where(last, second_cols, first_cols).astype(BF16)
        move_ref[rows, :] = jnp.where(last, first_cols, second_cols).astype(BF16)


def kernel(
    tour_hbm, y_hbm, out_ref,
    tour_ref, tour_sem,
    y_ref, kept, moving, arrived, moved, early_in, early_kept, side_in,
    keep_cols, move_cols, far_keep, far_move, acc, wide_in, narrow_out, narrow_in, gram_out, gram_in,
    load_sem, send_sem, recv_sem, ex_send, ex_recv, early_send, early_recv, side_send, side_recv,
):
    samp, pair = lax.axis_index("samp"), lax.axis_index("pair")
    slots = lax.axis_size("pair")
    half = slots // 2

    def slot(by):
        return lax.rem(pair + (by + slots), slots)

    ahead = {"pair": slot(half + 1)}
    side = {"pair": slot(2)}
    core_peer = {"samp": samp + 1 - 2 * lax.rem(samp, 2)}
    far_peer = {"samp": lax.rem(samp + 2, 4)}
    height, width = kept.shape
    low, high = pl.ds(0, width), pl.ds(width, width)
    early = pl.ds(0, EARLY)
    n_early, n_chunks = EARLY // CHUNK, height // CHUNK

    def rows_of(i, size=CHUNK):
        return pl.ds(pl.multiple_of(i * size, size), size)

    def stage(name):
        def run(body):
            with jax.named_scope(name):
                pl.when(samp >= 0)(body)

        return run

    def remote(source, target, send, recv, where):
        return pltpu.make_async_remote_copy(
            source, target, send, recv, device_id=where, device_id_type=MESH
        )

    n_loads = load_sem.shape[0]
    part = height // n_loads
    loads = [
        pltpu.make_async_copy(y_hbm.at[pl.ds(i * part, part)], y_ref.at[pl.ds(i * part, part)], load_sem.at[i])
        for i in range(n_loads)
    ]
    for load in loads:
        load.start()
    tour_load = pltpu.make_async_copy(tour_hbm, tour_ref, tour_sem)
    tour_load.start()
    barrier = pltpu.get_barrier_semaphore()
    greeted = (ahead, {"pair": slot(-half - 1)}, side, {"pair": slot(-2)}, core_peer, far_peer)
    for where in greeted:
        pl.semaphore_signal(barrier, inc=1, device_id=where, device_id_type=MESH)

    def summed_gram(step):
        near = remote(acc, wide_in.at[step], ex_send.at[4 * step], ex_recv.at[4 * step], core_peer)
        near.start()
        near.wait()
        chip = (acc[...] + wide_in[step]).astype(BF16)
        narrow_out[step] = chip
        far = remote(
            narrow_out.at[step], narrow_in.at[step], ex_send.at[4 * step + 1], ex_recv.at[4 * step + 1], far_peer
        )
        far.start()
        far.wait()
        total = (chip.astype(F32) + narrow_in[step].astype(F32)).astype(BF16)
        gram_out[step] = total
        passed_gram(step).start()
        if step == 0:
            early_move(1).start()

    core = lax.rem(samp, 2)
    my_part = pl.ds(pl.multiple_of(core * (width // 2), width // 2), width // 2)

    def passed_gram(step):
        source, target = gram_out.at[step, my_part], gram_in.at[step, my_part]
        return remote(source, target, ex_send.at[4 * step + 2], ex_recv.at[4 * step + 2], ahead)

    def gram_from_behind(step):
        passed_gram(step).wait()
        half_gram = gram_in.at[step, my_part]
        share = remote(half_gram, half_gram, ex_send.at[4 * step + 3], ex_recv.at[4 * step + 3], core_peer)
        share.start()
        share.wait()

    def early_move(k):
        rows = pl.ds(*PIECES[k])
        return remote(y_hbm.at[rows], early_in.at[rows], early_send.at[k], early_recv.at[k], ahead)

    side_move = remote(moving.at[early], side_in, side_send, side_recv, side)

    def first_move(i):
        return remote(moving.at[rows_of(i)], arrived.at[rows_of(i)], send_sem.at[0, i], recv_sem.at[0, i], ahead)

    def second_move(i):
        return remote(
            moved.at[rows_of(i)], out_ref.at[rows_of(i), high], send_sem.at[1, i], recv_sem.at[1, i], ahead
        )

    def rotate_first(from_ref, cols_ref, to_ref, rows):
        to_ref[rows, :] = mul(from_ref[rows, :], cols_ref[...]).astype(BF16)

    def rotate_second(kept_ref, moved_ref, cols_ref, to_ref, to_cols, rows):
        total = mul(kept_ref[rows, :], cols_ref[low, :]) + mul(moved_ref[rows, :], cols_ref[high, :])
        to_ref[rows, to_cols] = total.astype(BF16)

    with jax.named_scope("gram0"):
        acc[...] = jnp.zeros_like(acc)
        for i in range(n_loads):
            loads[i].wait()
            rows = pl.ds(i * part, part)
            acc[...] += over_rows(y_ref[rows, low], y_ref[rows, high])
            if i == 0:
                tour_load.wait()
                pl.semaphore_wait(barrier, len(greeted))
                early_move(0).start()

    @stage("exch0")
    def _():
        summed_gram(0)
    @stage("polar0")
    def _():
        rotation_into(gram_out.at[0], tour_ref[0, pair], keep_cols, move_cols)
    @stage("moves0")
    def _():

        @pl.loop(n_early, n_chunks)
        def _(i):
            rotate_first(y_ref, move_cols, moving, rows_of(i))
            first_move(i).start()

        rotate_first(y_ref, move_cols, moving, early)

        @pl.loop(0, height // TILE)
        def _(i):
            rotate_first(y_ref, keep_cols, kept, rows_of(i, TILE))

    @stage("gwait0")
    def _():
        gram_from_behind(0)
    @stage("farpolar0")
    def _():
        rotation_into(gram_in.at[0], tour_ref[0, slot(-half - 1)], far_keep, far_move)
    @stage("early")
    def _():
        for k in range(len(PIECES)):
            early_move(k).wait()
        rotate_first(early_in, far_keep, early_kept, early)
        rotate_first(early_in, far_move, arrived, early)
        acc[...] = over_rows(kept[early, :], arrived[early, :])

    @stage("gram1")
    def _():

        @pl.loop(n_early, n_chunks)
        def _(i):
            first_move(i).wait_recv()
            acc[...] += over_rows(kept[rows_of(i), :], arrived[rows_of(i), :])

    @stage("exch1")
    def _():
        side_move.start()
        summed_gram(1)
    @stage("polar1")
    def _():
        rotation_into(gram_out.at[1], tour_ref[1, slot(half)], keep_cols, move_cols)
    @stage("moves1")
    def _():

        @pl.loop(n_early, n_chunks)
        def _(i):
            rotate_second(kept, arrived, move_cols, moved, low, rows_of(i))
            second_move(i).start()

        @pl.loop(0, height // TILE)
        def _(i):
            rotate_second(kept, arrived, keep_cols, out_ref, low, rows_of(i, TILE))

    @stage("gwait1")
    def _():
        gram_from_behind(1)
    @stage("farpolar1")
    def _():
        rotation_into(gram_in.at[1], tour_ref[1, slot(-1)], far_keep, far_move)
    @stage("side")
    def _():
        side_move.wait()
        rotate_second(early_kept, side_in, far_move, out_ref, high, early)

    @stage("last")
    def _():

        @pl.loop(n_early, n_chunks)
        def _(i):
            first_move(i).wait_send()
            second_move(i).wait()


def shards(matrix, tournament):
    height, columns = matrix.shape
    width = columns // 2
    block = pltpu.VMEM((height, width), BF16)
    short = pltpu.VMEM((EARLY, width), BF16)
    cols = pltpu.VMEM((columns, width), BF16)
    grams = pltpu.VMEM((2, width, width), BF16)
    copies = pltpu.SemaphoreType.DMA((2, height // CHUNK))
    one = pltpu.SemaphoreType.DMA
    return pl.pallas_call(
        kernel,
        out_shape=pltpu.VMEM((height, columns), BF16),
        in_specs=[pl.BlockSpec(memory_space=pl.ANY), pl.BlockSpec(memory_space=pl.ANY)],
        out_specs=pl.BlockSpec(memory_space=pltpu.VMEM),
        scratch_shapes=[
            pltpu.SMEM(tournament.shape, jnp.int32), pltpu.SemaphoreType.DMA,
            pltpu.VMEM((height, columns), BF16), block, block, block, block,
            pltpu.VMEM((EARLY, columns), BF16), short, short, cols, cols, cols, cols,
            pltpu.VMEM((width, width), F32), pltpu.VMEM((2, width, width), F32), grams, grams, grams, grams,
            pltpu.SemaphoreType.DMA((4,)), copies, copies,
            pltpu.SemaphoreType.DMA((8,)), pltpu.SemaphoreType.DMA((8,)),
            one((len(PIECES),)), one((len(PIECES),)), one, one,
        ],
        compiler_params=pltpu.CompilerParams(
            collective_id=0, has_side_effects=True, vmem_limit_bytes=40 * 1024 * 1024
        ),
    )(tournament, matrix)


def solution(mesh):
    placed = (P("samp", "pair"), P())
    return jax.shard_map(
        shards, mesh=mesh, in_specs=placed, out_specs=P("samp", "pair"), check_vma=False
    )
```

```python
import jax
import jax.numpy as jnp
from jax import lax
from jax.experimental import pallas as pl
from jax.experimental.pallas import tpu as pltpu
from jax.sharding import PartitionSpec as P

POLAR_STEPS = 5
MESH = pl.DeviceIdType.MESH
COUPLING = 2.0
START_SCALE = 6.0
CHUNK = 128
TILE = 512
EARLY = 256
LATE = 128
PIECES = ((0, 128), (128, 128))
F32 = jnp.float32
BF16 = jnp.bfloat16


def over_rows(a, b):
    return lax.dot_general(a, b, (((0,), (0,)), ((), ())), preferred_element_type=F32)


def mul(a, b):
    return jnp.dot(a, b, preferred_element_type=F32)


def rotation_into(gram_ref, chosen, keep_ref, move_ref):
    gram = gram_ref[...].astype(F32)
    width = gram.shape[0]
    coupled = COUPLING * gram / jnp.sqrt(jnp.sum(gram * gram) + 1e-06)
    row = lax.broadcasted_iota(jnp.int32, (width, width), 0)
    eye = (row == lax.broadcasted_iota(jnp.int32, (width, width), 1)).astype(F32)
    halves = [jnp.concatenate([eye, -coupled], 1) / START_SCALE, jnp.concatenate([coupled.T, eye], 1) / START_SCALE]
    for _ in range(POLAR_STEPS):
        rounded = [h.astype(BF16) for h in halves]
        squares = [lax.dot_general(r, r, (((1,), (1,)), ((), ())), preferred_element_type=F32) for r in rounded]
        squares = [(-0.5 * q).astype(BF16) for q in squares]
        halves = [1.5 * h + mul(q, r) for h, q, r in zip(halves, squares, rounded)]
    last = chosen == 1
    for i, h in enumerate(halves):
        first_cols, second_cols = h[:, :width], h[:, width:]
        rows = pl.ds(i * width, width)
        keep_ref[rows, :] = jnp.where(last, second_cols, first_cols).astype(BF16)
        move_ref[rows, :] = jnp.where(last, first_cols, second_cols).astype(BF16)


def kernel(
    tour_hbm, y_hbm, out_ref,
    tour_ref, tour_sem,
    y_ref, kept, moving, arrived, moved, early_in, early_kept, side_in,
    keep_cols, move_cols, far_keep, far_move, acc, wide_in, narrow_out, narrow_in, gram_out, gram_in,
    load_sem, send_sem, recv_sem, ex_send, ex_recv, early_send, early_recv, side_send, side_recv,
):
    samp, pair = lax.axis_index("samp"), lax.axis_index("pair")
    slots = lax.axis_size("pair")
    half = slots // 2

    def slot(by):
        return lax.rem(pair + (by + slots), slots)

    ahead = {"pair": slot(half + 1)}
    side = {"pair": slot(2)}
    core_peer = {"samp": samp + 1 - 2 * lax.rem(samp, 2)}
    far_peer = {"samp": lax.rem(samp + 2, 4)}
    height, width = kept.shape
    low, high = pl.ds(0, width), pl.ds(width, width)
    early, late, aside = pl.ds(0, EARLY), pl.ds(EARLY, LATE), pl.ds(0, EARLY + LATE)
    n_early, n_aside, n_chunks = EARLY // CHUNK, (EARLY + LATE) // CHUNK, height // CHUNK

    def rows_of(i, size=CHUNK):
        return pl.ds(pl.multiple_of(i * size, size), size)

    def stage(name):
        def run(body):
            with jax.named_scope(name):
                pl.when(samp >= 0)(body)

        return run

    def remote(source, target, send, recv, where):
        return pltpu.make_async_remote_copy(
            source, target, send, recv, device_id=where, device_id_type=MESH
        )

    n_loads = load_sem.shape[0]
    load_rows = height // n_loads
    loads = [
        pltpu.make_async_copy(y_hbm.at[pl.ds(i * load_rows, load_rows)], y_ref.at[pl.ds(i * load_rows, load_rows)], load_sem.at[i])
        for i in range(n_loads)
    ]
    for load in loads:
        load.start()
    tour_load = pltpu.make_async_copy(tour_hbm, tour_ref, tour_sem)
    tour_load.start()
    barrier = pltpu.get_barrier_semaphore()
    greeted = (ahead, {"pair": slot(-half - 1)}, side, {"pair": slot(-2)}, core_peer, far_peer)
    for where in greeted:
        pl.semaphore_signal(barrier, inc=1, device_id=where, device_id_type=MESH)

    core = lax.rem(samp, 2)
    part = width // 2
    my_part = pl.ds(pl.multiple_of(core * part, part), part)
    peer_part = pl.ds(pl.multiple_of((1 - core) * part, part), part)

    def exchange(source, target, step, kind, where):
        n = kind + 5 * step
        return remote(source, target, ex_send.at[n], ex_recv.at[n], where)

    def passed_gram(step):
        return exchange(gram_out.at[step, my_part], gram_in.at[step, my_part], step, 2, ahead)

    def summed_gram(step):
        near = exchange(acc.at[peer_part], wide_in.at[step], step, 0, core_peer)
        near.start()
        near.wait()
        chip = (acc[my_part, :] + wide_in[step]).astype(BF16)
        narrow_out[step] = chip
        far = exchange(narrow_out.at[step], narrow_in.at[step], step, 1, far_peer)
        far.start()
        far.wait()
        gram_out[step, my_part] = (chip.astype(F32) + narrow_in[step].astype(F32)).astype(BF16)
        share = exchange(gram_out.at[step, my_part], gram_out.at[step, my_part], step, 3, core_peer)
        share.start()
        if step == 0:
            early_move(1).start()
        else:
            late_move.start()
        passed_gram(step).start()
        share.wait()

    def gram_from_behind(step):
        passed_gram(step).wait()
        half_gram = gram_in.at[step, my_part]
        share = exchange(half_gram, half_gram, step, 4, core_peer)
        share.start()
        share.wait()

    def early_move(k):
        rows = pl.ds(*PIECES[k])
        return remote(y_hbm.at[rows], early_in.at[rows], early_send.at[k], early_recv.at[k], ahead)

    side_move = remote(moving.at[aside], side_in, side_send.at[0], side_recv.at[0], side)
    late_move = remote(kept.at[late], early_kept.at[late], side_send.at[1], side_recv.at[1], ahead)

    def first_move(i):
        return remote(moving.at[rows_of(i)], arrived.at[rows_of(i)], send_sem.at[0, i], recv_sem.at[0, i], ahead)

    def second_move(i):
        return remote(
            moved.at[rows_of(i)], out_ref.at[rows_of(i), high], send_sem.at[1, i], recv_sem.at[1, i], ahead
        )

    def rotate_first(from_ref, cols_ref, to_ref, rows):
        to_ref[rows, :] = mul(from_ref[rows, :], cols_ref[...]).astype(BF16)

    def rotate_second(kept_ref, moved_ref, cols_ref, to_ref, to_cols, rows):
        total = mul(kept_ref[rows, :], cols_ref[low, :]) + mul(moved_ref[rows, :], cols_ref[high, :])
        to_ref[rows, to_cols] = total.astype(BF16)

    with jax.named_scope("gram0"):
        acc[...] = jnp.zeros_like(acc)
        for i in range(n_loads):
            loads[i].wait()
            rows = pl.ds(i * load_rows, load_rows)
            acc[...] += over_rows(y_ref[rows, low], y_ref[rows, high])
            if i == 0:
                tour_load.wait()
                pl.semaphore_wait(barrier, len(greeted))
                early_move(0).start()

    @stage("exch0")
    def _():
        summed_gram(0)
    @stage("polar0")
    def _():
        rotation_into(gram_out.at[0], tour_ref[0, pair], keep_cols, move_cols)
    @stage("moves0")
    def _():

        @pl.loop(n_early, n_chunks)
        def _(i):
            rotate_first(y_ref, move_cols, moving, rows_of(i))
            first_move(i).start()

        rotate_first(y_ref, move_cols, moving, early)

        @pl.loop(0, height // TILE)
        def _(i):
            rotate_first(y_ref, keep_cols, kept, rows_of(i, TILE))

    @stage("gwait0")
    def _():
        gram_from_behind(0)
    @stage("farpolar0")
    def _():
        rotation_into(gram_in.at[0], tour_ref[0, slot(-half - 1)], far_keep, far_move)
    @stage("early")
    def _():
        for k in range(len(PIECES)):
            early_move(k).wait()
        rotate_first(early_in, far_keep, early_kept, early)
        rotate_first(early_in, far_move, arrived, early)
        acc[...] = over_rows(kept[early, :], arrived[early, :])

    @stage("gram1")
    def _():

        @pl.loop(n_early, n_chunks)
        def _(i):
            first_move(i).wait_recv()
            acc[...] += over_rows(kept[rows_of(i), :], arrived[rows_of(i), :])

    @stage("exch1")
    def _():
        side_move.start()
        summed_gram(1)
    @stage("polar1")
    def _():
        rotation_into(gram_out.at[1], tour_ref[1, slot(half)], keep_cols, move_cols)
    @stage("moves1")
    def _():

        @pl.loop(n_aside, n_chunks)
        def _(i):
            rotate_second(kept, arrived, move_cols, moved, low, rows_of(i))
            second_move(i).start()

        @pl.loop(0, height // TILE)
        def _(i):
            rotate_second(kept, arrived, keep_cols, out_ref, low, rows_of(i, TILE))

    @stage("gwait1")
    def _():
        gram_from_behind(1)
    @stage("farpolar1")
    def _():
        rotation_into(gram_in.at[1], tour_ref[1, slot(-1)], far_keep, far_move)
    @stage("side")
    def _():
        side_move.wait()
        late_move.wait()
        rotate_second(early_kept, side_in, far_move, out_ref, high, aside)

    @stage("last")
    def _():

        @pl.loop(n_early, n_chunks)
        def _(i):
            first_move(i).wait_send()

        @pl.loop(n_aside, n_chunks)
        def _(i):
            second_move(i).wait()


def shards(matrix, tournament):
    height, columns = matrix.shape
    width = columns // 2
    block = pltpu.VMEM((height, width), BF16)
    short = pltpu.VMEM((EARLY + LATE, width), BF16)
    cols = pltpu.VMEM((columns, width), BF16)
    grams = pltpu.VMEM((2, width, width), BF16)
    halves = pltpu.VMEM((2, width // 2, width), BF16)
    copies = pltpu.SemaphoreType.DMA((2, height // CHUNK))
    one = pltpu.SemaphoreType.DMA
    return pl.pallas_call(
        kernel,
        out_shape=pltpu.VMEM((height, columns), BF16),
        in_specs=[pl.BlockSpec(memory_space=pltpu.HBM), pl.BlockSpec(memory_space=pl.ANY)],
        out_specs=pl.BlockSpec(memory_space=pltpu.VMEM),
        scratch_shapes=[
            pltpu.SMEM(tournament.shape, jnp.int32), pltpu.SemaphoreType.DMA,
            pltpu.VMEM((height, columns), BF16), block, block, block, block,
            pltpu.VMEM((EARLY, columns), BF16), short, short, cols, cols, cols, cols,
            pltpu.VMEM((width, width), F32), pltpu.VMEM((2, width // 2, width), F32), halves, halves, grams, grams,
            pltpu.SemaphoreType.DMA((4,)), copies, copies,
            pltpu.SemaphoreType.DMA((10,)), pltpu.SemaphoreType.DMA((10,)),
            one((len(PIECES),)), one((len(PIECES),)), one((2,)), one((2,)),
        ],
        compiler_params=pltpu.CompilerParams(
            collective_id=0, has_side_effects=True, vmem_limit_bytes=40 * 1024 * 1024
        ),
    )(tournament, matrix)


def solution(mesh):
    placed = (P("samp", "pair"), P())
    return jax.shard_map(
        shards, mesh=mesh, in_specs=placed, out_specs=P("samp", "pair"), check_vma=False
    )
```

```python
import jax
import jax.numpy as jnp
from jax import lax
from jax.experimental import pallas as pl
from jax.experimental.pallas import tpu as pltpu
from jax.sharding import PartitionSpec as P

POLAR_STEPS = 5
MESH = pl.DeviceIdType.MESH
COUPLING = 2.0
START_SCALE = 6.0
CHUNK = 128
TILE = 512
EARLY = 256
LATE = 256
PIECES = ((0, 128), (128, 128))
F32 = jnp.float32
BF16 = jnp.bfloat16


def over_rows(a, b):
    return lax.dot_general(a, b, (((0,), (0,)), ((), ())), preferred_element_type=F32)


def mul(a, b):
    return jnp.dot(a, b, preferred_element_type=F32)


def rotation_into(gram_ref, chosen, keep_ref, move_ref):
    gram = gram_ref[...].astype(F32)
    width = gram.shape[0]
    coupled = COUPLING * gram / jnp.sqrt(jnp.sum(gram * gram) + 1e-06)
    row = lax.broadcasted_iota(jnp.int32, (width, width), 0)
    eye = (row == lax.broadcasted_iota(jnp.int32, (width, width), 1)).astype(F32)
    halves = [jnp.concatenate([eye, -coupled], 1) / START_SCALE, jnp.concatenate([coupled.T, eye], 1) / START_SCALE]
    for _ in range(POLAR_STEPS):
        rounded = [h.astype(BF16) for h in halves]
        squares = [lax.dot_general(r, r, (((1,), (1,)), ((), ())), preferred_element_type=F32) for r in rounded]
        squares = [(-0.5 * q).astype(BF16) for q in squares]
        halves = [1.5 * h + mul(q, r) for h, q, r in zip(halves, squares, rounded)]
    last = chosen == 1
    for i, h in enumerate(halves):
        first_cols, second_cols = h[:, :width], h[:, width:]
        rows = pl.ds(i * width, width)
        keep_ref[rows, :] = jnp.where(last, second_cols, first_cols).astype(BF16)
        move_ref[rows, :] = jnp.where(last, first_cols, second_cols).astype(BF16)


def kernel(
    tour_hbm, y_hbm, out_ref,
    tour_ref, tour_sem,
    y_ref, kept, moving, arrived, moved, early_in, early_kept, side_in,
    keep_cols, move_cols, far_keep, far_move, acc, wide_in, narrow_out, narrow_in, gram_out, gram_in,
    load_sem, send_sem, recv_sem, ex_send, ex_recv, early_send, early_recv, side_send, side_recv,
):
    samp, pair = lax.axis_index("samp"), lax.axis_index("pair")
    slots = lax.axis_size("pair")
    half = slots // 2

    def slot(by):
        return lax.rem(pair + (by + slots), slots)

    ahead = {"pair": slot(half + 1)}
    side = {"pair": slot(2)}
    core_peer = {"samp": samp + 1 - 2 * lax.rem(samp, 2)}
    far_peer = {"samp": lax.rem(samp + 2, 4)}
    height, width = kept.shape
    low, high = pl.ds(0, width), pl.ds(width, width)
    early, aside = pl.ds(0, EARLY), pl.ds(0, EARLY + LATE)
    n_early, n_aside, n_chunks = EARLY // CHUNK, (EARLY + LATE) // CHUNK, height // CHUNK

    def rows_of(i, size=CHUNK):
        return pl.ds(pl.multiple_of(i * size, size), size)

    def stage(name):
        def run(body):
            with jax.named_scope(name):
                pl.when(samp >= 0)(body)

        return run

    def remote(source, target, send, recv, where):
        return pltpu.make_async_remote_copy(
            source, target, send, recv, device_id=where, device_id_type=MESH
        )

    n_loads = load_sem.shape[0]
    load_rows = height // n_loads
    loads = [
        pltpu.make_async_copy(y_hbm.at[pl.ds(i * load_rows, load_rows)], y_ref.at[pl.ds(i * load_rows, load_rows)], load_sem.at[i])
        for i in range(n_loads)
    ]
    for load in loads:
        load.start()
    tour_load = pltpu.make_async_copy(tour_hbm, tour_ref, tour_sem)
    tour_load.start()
    barrier = pltpu.get_barrier_semaphore()
    greeted = (ahead, {"pair": slot(-half - 1)}, side, {"pair": slot(-2)}, core_peer, far_peer)
    for where in greeted:
        pl.semaphore_signal(barrier, inc=1, device_id=where, device_id_type=MESH)

    core = lax.rem(samp, 2)
    part = width // 2
    my_part = pl.ds(pl.multiple_of(core * part, part), part)
    peer_part = pl.ds(pl.multiple_of((1 - core) * part, part), part)

    def exchange(source, target, step, kind, where):
        n = kind + 5 * step
        return remote(source, target, ex_send.at[n], ex_recv.at[n], where)

    def passed_gram(step):
        return exchange(gram_out.at[step, my_part], gram_in.at[step, my_part], step, 2, ahead)

    def summed_gram(step):
        near = exchange(acc.at[peer_part], wide_in.at[step], step, 0, core_peer)
        near.start()
        near.wait()
        chip = (acc[my_part, :] + wide_in[step]).astype(BF16)
        narrow_out[step] = chip
        far = exchange(narrow_out.at[step], narrow_in.at[step], step, 1, far_peer)
        far.start()
        far.wait()
        gram_out[step, my_part] = (chip.astype(F32) + narrow_in[step].astype(F32)).astype(BF16)
        share = exchange(gram_out.at[step, my_part], gram_out.at[step, my_part], step, 3, core_peer)
        share.start()
        if step == 0:
            early_move(1).start()
        else:
            late_move(1).start()
        passed_gram(step).start()
        share.wait()

    def gram_from_behind(step):
        passed_gram(step).wait()
        half_gram = gram_in.at[step, my_part]
        share = exchange(half_gram, half_gram, step, 4, core_peer)
        share.start()
        share.wait()

    def early_move(k):
        rows = pl.ds(*PIECES[k])
        return remote(y_hbm.at[rows], early_in.at[rows], early_send.at[k], early_recv.at[k], ahead)

    side_move = remote(moving.at[aside], side_in, side_send.at[0], side_recv.at[0], side)

    def late_move(k):
        rows = pl.ds(EARLY + k * (LATE // 2), LATE // 2)
        return remote(kept.at[rows], early_kept.at[rows], side_send.at[1 + k], side_recv.at[1 + k], ahead)

    def first_move(i):
        return remote(moving.at[rows_of(i)], arrived.at[rows_of(i)], send_sem.at[0, i], recv_sem.at[0, i], ahead)

    def second_move(i):
        return remote(
            moved.at[rows_of(i)], out_ref.at[rows_of(i), high], send_sem.at[1, i], recv_sem.at[1, i], ahead
        )

    def rotate_first(from_ref, cols_ref, to_ref, rows):
        to_ref[rows, :] = mul(from_ref[rows, :], cols_ref[...]).astype(BF16)

    def rotate_second(kept_ref, moved_ref, cols_ref, to_ref, to_cols, rows):
        total = mul(kept_ref[rows, :], cols_ref[low, :]) + mul(moved_ref[rows, :], cols_ref[high, :])
        to_ref[rows, to_cols] = total.astype(BF16)

    with jax.named_scope("gram0"):
        acc[...] = jnp.zeros_like(acc)
        for i in range(n_loads):
            loads[i].wait()
            rows = pl.ds(i * load_rows, load_rows)
            acc[...] += over_rows(y_ref[rows, low], y_ref[rows, high])
            if i == 0:
                tour_load.wait()
                pl.semaphore_wait(barrier, len(greeted))
                early_move(0).start()

    @stage("exch0")
    def _():
        summed_gram(0)
    @stage("polar0")
    def _():
        rotation_into(gram_out.at[0], tour_ref[0, pair], keep_cols, move_cols)
    @stage("moves0")
    def _():

        @pl.loop(n_early, n_chunks)
        def _(i):
            rotate_first(y_ref, move_cols, moving, rows_of(i))
            first_move(i).start()

        rotate_first(y_ref, move_cols, moving, early)

        @pl.loop(0, height // TILE)
        def _(i):
            rotate_first(y_ref, keep_cols, kept, rows_of(i, TILE))

        late_move(0).start()

    @stage("gwait0")
    def _():
        gram_from_behind(0)
    @stage("farpolar0")
    def _():
        rotation_into(gram_in.at[0], tour_ref[0, slot(-half - 1)], far_keep, far_move)
    @stage("early")
    def _():
        for k in range(len(PIECES)):
            early_move(k).wait()
        rotate_first(early_in, far_keep, early_kept, early)
        rotate_first(early_in, far_move, arrived, early)
        acc[...] = over_rows(kept[early, :], arrived[early, :])

    @stage("gram1")
    def _():

        @pl.loop(n_early, n_chunks)
        def _(i):
            first_move(i).wait_recv()
            acc[...] += over_rows(kept[rows_of(i), :], arrived[rows_of(i), :])

    @stage("exch1")
    def _():
        side_move.start()
        summed_gram(1)
    @stage("polar1")
    def _():
        rotation_into(gram_out.at[1], tour_ref[1, slot(half)], keep_cols, move_cols)
    @stage("moves1")
    def _():

        @pl.loop(n_aside, n_chunks)
        def _(i):
            rotate_second(kept, arrived, move_cols, moved, low, rows_of(i))
            second_move(i).start()

        @pl.loop(0, height // TILE)
        def _(i):
            rotate_second(kept, arrived, keep_cols, out_ref, low, rows_of(i, TILE))

    @stage("gwait1")
    def _():
        gram_from_behind(1)
    @stage("farpolar1")
    def _():
        rotation_into(gram_in.at[1], tour_ref[1, slot(-1)], far_keep, far_move)
    @stage("side")
    def _():
        side_move.wait()
        late_move(0).wait()
        late_move(1).wait()
        rotate_second(early_kept, side_in, far_move, out_ref, high, aside)

    @stage("last")
    def _():

        @pl.loop(n_early, n_chunks)
        def _(i):
            first_move(i).wait_send()

        @pl.loop(n_aside, n_chunks)
        def _(i):
            second_move(i).wait()


def shards(matrix, tournament):
    height, columns = matrix.shape
    width = columns // 2
    block = pltpu.VMEM((height, width), BF16)
    short = pltpu.VMEM((EARLY + LATE, width), BF16)
    cols = pltpu.VMEM((columns, width), BF16)
    grams = pltpu.VMEM((2, width, width), BF16)
    halves = pltpu.VMEM((2, width // 2, width), BF16)
    copies = pltpu.SemaphoreType.DMA((2, height // CHUNK))
    one = pltpu.SemaphoreType.DMA
    return pl.pallas_call(
        kernel,
        out_shape=pltpu.VMEM((height, columns), BF16),
        in_specs=[pl.BlockSpec(memory_space=pltpu.HBM), pl.BlockSpec(memory_space=pl.ANY)],
        out_specs=pl.BlockSpec(memory_space=pltpu.VMEM),
        scratch_shapes=[
            pltpu.SMEM(tournament.shape, jnp.int32), pltpu.SemaphoreType.DMA,
            pltpu.VMEM((height, columns), BF16), block, block, block, block,
            pltpu.VMEM((EARLY, columns), BF16), short, short, cols, cols, cols, cols,
            pltpu.VMEM((width, width), F32), pltpu.VMEM((2, width // 2, width), F32), halves, halves, grams, grams,
            pltpu.SemaphoreType.DMA((4,)), copies, copies,
            pltpu.SemaphoreType.DMA((10,)), pltpu.SemaphoreType.DMA((10,)),
            one((len(PIECES),)), one((len(PIECES),)), one((3,)), one((3,)),
        ],
        compiler_params=pltpu.CompilerParams(
            collective_id=0, has_side_effects=True, vmem_limit_bytes=56_000_000
        ),
    )(tournament, matrix)


def solution(mesh):
    placed = (P("samp", "pair"), P())
    return jax.shard_map(
        shards, mesh=mesh, in_specs=placed, out_specs=P("samp", "pair"), check_vma=False
    )
```

```python
import jax
import jax.numpy as jnp
from jax import lax
from jax.experimental import pallas as pl
from jax.experimental.pallas import tpu as pltpu
from jax.sharding import PartitionSpec as P

POLAR_STEPS = 5
MESH = pl.DeviceIdType.MESH
COUPLING = 2.0
START_SCALE = 6.0
CHUNK = 512
TILE = 512
EARLY = 256
LATE = 256
PIECES = ((0, 128), (128, 128))
F32 = jnp.float32
BF16 = jnp.bfloat16


def over_rows(a, b):
    return lax.dot_general(a, b, (((0,), (0,)), ((), ())), preferred_element_type=F32)


def mul(a, b):
    return jnp.dot(a, b, preferred_element_type=F32)


def rotation_into(gram_ref, chosen, keep_ref, move_ref):
    gram = gram_ref[...].astype(F32)
    width = gram.shape[0]
    coupled = COUPLING * gram / jnp.sqrt(jnp.sum(gram * gram) + 1e-06)
    row = lax.broadcasted_iota(jnp.int32, (width, width), 0)
    eye = (row == lax.broadcasted_iota(jnp.int32, (width, width), 1)).astype(F32)
    halves = [jnp.concatenate([eye, -coupled], 1) / START_SCALE, jnp.concatenate([coupled.T, eye], 1) / START_SCALE]
    for _ in range(POLAR_STEPS):
        rounded = [h.astype(BF16) for h in halves]
        squares = [lax.dot_general(r, r, (((1,), (1,)), ((), ())), preferred_element_type=F32) for r in rounded]
        squares = [(-0.5 * q).astype(BF16) for q in squares]
        halves = [1.5 * h + mul(q, r) for h, q, r in zip(halves, squares, rounded)]
    last = chosen == 1
    for i, h in enumerate(halves):
        first_cols, second_cols = h[:, :width], h[:, width:]
        rows = pl.ds(i * width, width)
        keep_ref[rows, :] = jnp.where(last, second_cols, first_cols).astype(BF16)
        move_ref[rows, :] = jnp.where(last, first_cols, second_cols).astype(BF16)


def kernel(
    tour_hbm, y_hbm, out_ref,
    tour_ref, tour_sem,
    y_ref, kept, moving, arrived, moved, early_in, early_kept, side_in,
    keep_cols, move_cols, far_keep, far_move, acc, wide_in, narrow_out, narrow_in, gram_out, gram_in,
    load_sem, send_sem, recv_sem, ex_send, ex_recv, early_send, early_recv, side_send, side_recv,
):
    samp, pair = lax.axis_index("samp"), lax.axis_index("pair")
    slots = lax.axis_size("pair")
    half = slots // 2

    def slot(by):
        return lax.rem(pair + (by + slots), slots)

    ahead = {"pair": slot(half + 1)}
    side = {"pair": slot(2)}
    core_peer = {"samp": samp + 1 - 2 * lax.rem(samp, 2)}
    far_peer = {"samp": lax.rem(samp + 2, 4)}
    height, width = kept.shape
    low, high = pl.ds(0, width), pl.ds(width, width)
    early, aside = pl.ds(0, EARLY), pl.ds(0, EARLY + LATE)
    n_aside, n_chunks = (EARLY + LATE) // CHUNK, height // CHUNK
    head = pl.ds(EARLY, LATE)

    def rows_of(i, size=CHUNK):
        return pl.ds(pl.multiple_of(i * size, size), size)

    def stage(name):
        def run(body):
            with jax.named_scope(name):
                pl.when(samp >= 0)(body)

        return run

    def remote(source, target, send, recv, where):
        return pltpu.make_async_remote_copy(
            source, target, send, recv, device_id=where, device_id_type=MESH
        )

    n_loads = load_sem.shape[0]
    load_rows = height // n_loads
    loads = [
        pltpu.make_async_copy(y_hbm.at[pl.ds(i * load_rows, load_rows)], y_ref.at[pl.ds(i * load_rows, load_rows)], load_sem.at[i])
        for i in range(n_loads)
    ]
    for load in loads:
        load.start()
    tour_load = pltpu.make_async_copy(tour_hbm, tour_ref, tour_sem)
    tour_load.start()
    barrier = pltpu.get_barrier_semaphore()
    greeted = (ahead, {"pair": slot(-half - 1)}, side, {"pair": slot(-2)}, core_peer, far_peer)
    for where in greeted:
        pl.semaphore_signal(barrier, inc=1, device_id=where, device_id_type=MESH)

    core = lax.rem(samp, 2)
    part = width // 2
    my_part = pl.ds(pl.multiple_of(core * part, part), part)
    peer_part = pl.ds(pl.multiple_of((1 - core) * part, part), part)

    def exchange(source, target, step, kind, where):
        n = kind + 5 * step
        return remote(source, target, ex_send.at[n], ex_recv.at[n], where)

    def passed_gram(step):
        return exchange(gram_out.at[step, my_part], gram_in.at[step, my_part], step, 2, ahead)

    def summed_gram(step):
        near = exchange(acc.at[peer_part], wide_in.at[step], step, 0, core_peer)
        near.start()
        near.wait()
        chip = (acc[my_part, :] + wide_in[step]).astype(BF16)
        narrow_out[step] = chip
        far = exchange(narrow_out.at[step], narrow_in.at[step], step, 1, far_peer)
        far.start()
        far.wait()
        gram_out[step, my_part] = (chip.astype(F32) + narrow_in[step].astype(F32)).astype(BF16)
        share = exchange(gram_out.at[step, my_part], gram_out.at[step, my_part], step, 3, core_peer)
        share.start()
        if step == 0:
            early_move(1).start()
        else:
            late_move(1).start()
        passed_gram(step).start()
        share.wait()

    def gram_from_behind(step):
        passed_gram(step).wait()
        half_gram = gram_in.at[step, my_part]
        share = exchange(half_gram, half_gram, step, 4, core_peer)
        share.start()
        share.wait()

    def early_move(k):
        rows = pl.ds(*PIECES[k])
        return remote(y_hbm.at[rows], early_in.at[rows], early_send.at[k], early_recv.at[k], ahead)

    side_move = remote(moving.at[aside], side_in, side_send.at[0], side_recv.at[0], side)

    def late_move(k):
        rows = pl.ds(EARLY + k * (LATE // 2), LATE // 2)
        return remote(kept.at[rows], early_kept.at[rows], side_send.at[1 + k], side_recv.at[1 + k], ahead)

    def first_move(i, rows=None):
        rows = rows_of(i) if rows is None else rows
        return remote(moving.at[rows], arrived.at[rows], send_sem.at[0, i], recv_sem.at[0, i], ahead)

    head_move = first_move(0, head)

    def second_move(i):
        return remote(
            moved.at[rows_of(i)], out_ref.at[rows_of(i), high], send_sem.at[1, i], recv_sem.at[1, i], ahead
        )

    def rotate_first(from_ref, cols_ref, to_ref, rows):
        to_ref[rows, :] = mul(from_ref[rows, :], cols_ref[...]).astype(BF16)

    def rotate_second(kept_ref, moved_ref, cols_ref, to_ref, to_cols, rows):
        total = mul(kept_ref[rows, :], cols_ref[low, :]) + mul(moved_ref[rows, :], cols_ref[high, :])
        to_ref[rows, to_cols] = total.astype(BF16)

    with jax.named_scope("gram0"):
        acc[...] = jnp.zeros_like(acc)
        for i in range(n_loads):
            loads[i].wait()
            rows = pl.ds(i * load_rows, load_rows)
            acc[...] += over_rows(y_ref[rows, low], y_ref[rows, high])
            if i == 0:
                tour_load.wait()
                pl.semaphore_wait(barrier, len(greeted))
                early_move(0).start()

    @stage("exch0")
    def _():
        summed_gram(0)
    @stage("polar0")
    def _():
        rotation_into(gram_out.at[0], tour_ref[0, pair], keep_cols, move_cols)
    @stage("moves0")
    def _():

        rotate_first(y_ref, move_cols, moving, head)
        head_move.start()

        @pl.loop(n_aside, n_chunks)
        def _(i):
            rotate_first(y_ref, move_cols, moving, rows_of(i))
            first_move(i).start()

        rotate_first(y_ref, move_cols, moving, early)

        @pl.loop(0, height // TILE)
        def _(i):
            rotate_first(y_ref, keep_cols, kept, rows_of(i, TILE))

        late_move(0).start()

    @stage("gwait0")
    def _():
        gram_from_behind(0)
    @stage("farpolar0")
    def _():
        rotation_into(gram_in.at[0], tour_ref[0, slot(-half - 1)], far_keep, far_move)
    @stage("early")
    def _():
        for k in range(len(PIECES)):
            early_move(k).wait()
        rotate_first(early_in, far_keep, early_kept, early)
        rotate_first(early_in, far_move, arrived, early)
        acc[...] = over_rows(kept[early, :], arrived[early, :])

    @stage("gram1")
    def _():

        head_move.wait_recv()
        acc[...] += over_rows(kept[head, :], arrived[head, :])

        @pl.loop(n_aside, n_chunks)
        def _(i):
            first_move(i).wait_recv()
            acc[...] += over_rows(kept[rows_of(i), :], arrived[rows_of(i), :])

    @stage("exch1")
    def _():
        side_move.start()
        summed_gram(1)
    @stage("polar1")
    def _():
        rotation_into(gram_out.at[1], tour_ref[1, slot(half)], keep_cols, move_cols)
    @stage("moves1")
    def _():

        @pl.loop(n_aside, n_chunks)
        def _(i):
            rotate_second(kept, arrived, move_cols, moved, low, rows_of(i))
            second_move(i).start()

        @pl.loop(0, height // TILE)
        def _(i):
            rotate_second(kept, arrived, keep_cols, out_ref, low, rows_of(i, TILE))

    @stage("gwait1")
    def _():
        gram_from_behind(1)
    @stage("farpolar1")
    def _():
        rotation_into(gram_in.at[1], tour_ref[1, slot(-1)], far_keep, far_move)
    @stage("side")
    def _():
        side_move.wait()
        late_move(0).wait()
        late_move(1).wait()
        rotate_second(early_kept, side_in, far_move, out_ref, high, aside)

    @stage("last")
    def _():

        head_move.wait_send()

        @pl.loop(n_aside, n_chunks)
        def _(i):
            first_move(i).wait_send()
            second_move(i).wait()


def shards(matrix, tournament):
    height, columns = matrix.shape
    width = columns // 2
    block = pltpu.VMEM((height, width), BF16)
    short = pltpu.VMEM((EARLY + LATE, width), BF16)
    cols = pltpu.VMEM((columns, width), BF16)
    grams = pltpu.VMEM((2, width, width), BF16)
    halves = pltpu.VMEM((2, width // 2, width), BF16)
    copies = pltpu.SemaphoreType.DMA((2, height // CHUNK))
    one = pltpu.SemaphoreType.DMA
    return pl.pallas_call(
        kernel,
        out_shape=pltpu.VMEM((height, columns), BF16),
        in_specs=[pl.BlockSpec(memory_space=pltpu.HBM), pl.BlockSpec(memory_space=pl.ANY)],
        out_specs=pl.BlockSpec(memory_space=pltpu.VMEM),
        scratch_shapes=[
            pltpu.SMEM(tournament.shape, jnp.int32), pltpu.SemaphoreType.DMA,
            pltpu.VMEM((height, columns), BF16), block, block, block, block,
            pltpu.VMEM((EARLY, columns), BF16), short, short, cols, cols, cols, cols,
            pltpu.VMEM((width, width), F32), pltpu.VMEM((2, width // 2, width), F32), halves, halves, grams, grams,
            pltpu.SemaphoreType.DMA((4,)), copies, copies,
            pltpu.SemaphoreType.DMA((10,)), pltpu.SemaphoreType.DMA((10,)),
            one((len(PIECES),)), one((len(PIECES),)), one((3,)), one((3,)),
        ],
        compiler_params=pltpu.CompilerParams(
            collective_id=0, has_side_effects=True, vmem_limit_bytes=56_000_000
        ),
    )(tournament, matrix)


def solution(mesh):
    placed = (P("samp", "pair"), P())
    return jax.shard_map(
        shards, mesh=mesh, in_specs=placed, out_specs=P("samp", "pair"), check_vma=False
    )
```

```python
import jax
import jax.numpy as jnp
from jax import lax
from jax.experimental import pallas as pl
from jax.experimental.pallas import tpu as pltpu
from jax.sharding import PartitionSpec as P

POLAR_STEPS = 5
MESH = pl.DeviceIdType.MESH
COUPLING = 2.0
START_SCALE = 6.0
CHUNK = 512
TILE = 512
EARLY = 256
LATE = 256
PIECES = ((0, 128), (128, 128))
F32 = jnp.float32
BF16 = jnp.bfloat16


def over_rows(a, b):
    return lax.dot_general(a, b, (((0,), (0,)), ((), ())), preferred_element_type=F32)


def mul(a, b):
    return jnp.dot(a, b, preferred_element_type=F32)


def rotation_into(gram_ref, chosen, keep_ref, move_ref):
    gram = gram_ref[...].astype(F32)
    width = gram.shape[0]
    coupled = COUPLING * gram / jnp.sqrt(jnp.sum(gram * gram) + 1e-06)
    row = lax.broadcasted_iota(jnp.int32, (width, width), 0)
    eye = (row == lax.broadcasted_iota(jnp.int32, (width, width), 1)).astype(F32)
    halves = [jnp.concatenate([eye, -coupled], 1) / START_SCALE, jnp.concatenate([coupled.T, eye], 1) / START_SCALE]
    for _ in range(POLAR_STEPS):
        rounded = [h.astype(BF16) for h in halves]
        squares = [lax.dot_general(r, r, (((1,), (1,)), ((), ())), preferred_element_type=F32) for r in rounded]
        squares = [(-0.5 * q).astype(BF16) for q in squares]
        halves = [1.5 * h + mul(q, r) for h, q, r in zip(halves, squares, rounded)]
    last = chosen == 1
    for i, h in enumerate(halves):
        first_cols, second_cols = h[:, :width], h[:, width:]
        rows = pl.ds(i * width, width)
        keep_ref[rows, :] = jnp.where(last, second_cols, first_cols).astype(BF16)
        move_ref[rows, :] = jnp.where(last, first_cols, second_cols).astype(BF16)


def kernel(
    tour_hbm, y_hbm, out_ref,
    tour_ref, tour_sem,
    y_ref, kept, moving, arrived, moved, early_in, early_kept, side_in,
    keep_cols, move_cols, far_keep, far_move, acc, wide_in, narrow_out, narrow_in, gram_out, gram_in,
    load_sem, send_sem, recv_sem, ex_send, ex_recv, early_send, early_recv, side_send, side_recv,
):
    samp, pair = lax.axis_index("samp"), lax.axis_index("pair")
    slots = lax.axis_size("pair")
    half = slots // 2

    def slot(by):
        return lax.rem(pair + (by + slots), slots)

    ahead = {"pair": slot(half + 1)}
    side = {"pair": slot(2)}
    core_peer = {"samp": samp + 1 - 2 * lax.rem(samp, 2)}
    far_peer = {"samp": lax.rem(samp + 2, 4)}
    height, width = kept.shape
    low, high = pl.ds(0, width), pl.ds(width, width)
    early, aside = pl.ds(0, EARLY), pl.ds(0, EARLY + LATE)
    n_aside, n_chunks = (EARLY + LATE) // CHUNK, height // CHUNK
    head = pl.ds(EARLY, LATE)

    def rows_of(i, size=CHUNK):
        return pl.ds(pl.multiple_of(i * size, size), size)

    def stage(name):
        def run(body):
            with jax.named_scope(name):
                pl.when(samp >= 0)(body)

        return run

    def remote(source, target, send, recv, where):
        return pltpu.make_async_remote_copy(
            source, target, send, recv, device_id=where, device_id_type=MESH
        )

    n_loads = load_sem.shape[0]
    load_rows = height // n_loads
    loads = [
        pltpu.make_async_copy(y_hbm.at[pl.ds(i * load_rows, load_rows)], y_ref.at[pl.ds(i * load_rows, load_rows)], load_sem.at[i])
        for i in range(n_loads)
    ]
    for load in loads:
        load.start()
    tour_load = pltpu.make_async_copy(tour_hbm, tour_ref, tour_sem)
    tour_load.start()
    barrier = pltpu.get_barrier_semaphore()
    greeted = (ahead, {"pair": slot(-half - 1)}, side, {"pair": slot(-2)}, core_peer, far_peer)
    for where in greeted:
        pl.semaphore_signal(barrier, inc=1, device_id=where, device_id_type=MESH)

    core = lax.rem(samp, 2)
    part = width // 2
    my_part = pl.ds(pl.multiple_of(core * part, part), part)
    peer_part = pl.ds(pl.multiple_of((1 - core) * part, part), part)

    def exchange(source, target, step, kind, where):
        n = kind + 5 * step
        return remote(source, target, ex_send.at[n], ex_recv.at[n], where)

    def passed_gram(step):
        return exchange(gram_out.at[step, my_part], gram_in.at[step, my_part], step, 2, ahead)

    def summed_gram(step):
        near = exchange(acc.at[peer_part], wide_in.at[step], step, 0, core_peer)
        near.start()
        near.wait()
        chip = (acc[my_part, :] + wide_in[step]).astype(BF16)
        narrow_out[step] = chip
        far = exchange(narrow_out.at[step], narrow_in.at[step], step, 1, far_peer)
        far.start()
        far.wait()
        gram_out[step, my_part] = (chip.astype(F32) + narrow_in[step].astype(F32)).astype(BF16)
        share = exchange(gram_out.at[step, my_part], gram_out.at[step, my_part], step, 3, core_peer)
        share.start()
        if step == 0:
            early_move(1).start()
        else:
            late_move(1).start()
        passed_gram(step).start()
        share.wait()

    def gram_from_behind(step):
        passed_gram(step).wait()
        half_gram = gram_in.at[step, my_part]
        share = exchange(half_gram, half_gram, step, 4, core_peer)
        share.start()
        share.wait()

    def early_move(k):
        rows = pl.ds(*PIECES[k])
        return remote(y_hbm.at[rows], early_in.at[rows], early_send.at[k], early_recv.at[k], ahead)

    side_move = remote(moving.at[aside], side_in, side_send.at[0], side_recv.at[0], side)

    def late_move(k):
        rows = pl.ds(EARLY + k * (LATE // 2), LATE // 2)
        return remote(kept.at[rows], early_kept.at[rows], side_send.at[1 + k], side_recv.at[1 + k], ahead)

    def first_move(i, rows=None):
        rows = rows_of(i) if rows is None else rows
        return remote(moving.at[rows], arrived.at[rows], send_sem.at[0, i], recv_sem.at[0, i], ahead)

    head_move = first_move(0, head)

    def second_move(i):
        return remote(
            moved.at[rows_of(i)], out_ref.at[rows_of(i), high], send_sem.at[1, i], recv_sem.at[1, i], ahead
        )

    def rotate_first(from_ref, cols_ref, to_ref, rows):
        to_ref[rows, :] = mul(from_ref[rows, :], cols_ref[...]).astype(BF16)

    def rotate_second(kept_ref, moved_ref, cols_ref, to_ref, to_cols, rows):
        total = mul(kept_ref[rows, :], cols_ref[low, :]) + mul(moved_ref[rows, :], cols_ref[high, :])
        to_ref[rows, to_cols] = total.astype(BF16)

    with jax.named_scope("gram0"):
        acc[...] = jnp.zeros_like(acc)
        for i in range(n_loads):
            loads[i].wait()
            if i < n_loads - 2 and i % 2 == 0:
                continue
            joined = 2 if i < n_loads - 2 else 1
            rows = pl.ds((i + 1 - joined) * load_rows, joined * load_rows)
            acc[...] += over_rows(y_ref[rows, low], y_ref[rows, high])
            if i == 1:
                tour_load.wait()
                pl.semaphore_wait(barrier, len(greeted))
                early_move(0).start()

    @stage("exch0")
    def _():
        summed_gram(0)
    @stage("polar0")
    def _():
        rotation_into(gram_out.at[0], tour_ref[0, pair], keep_cols, move_cols)
    @stage("moves0")
    def _():

        rotate_first(y_ref, move_cols, moving, head)
        head_move.start()

        @pl.loop(n_aside, n_chunks)
        def _(i):
            rotate_first(y_ref, move_cols, moving, rows_of(i))
            first_move(i).start()

        rotate_first(y_ref, move_cols, moving, early)

        @pl.loop(0, height // TILE)
        def _(i):
            rotate_first(y_ref, keep_cols, kept, rows_of(i, TILE))

        late_move(0).start()

    @stage("gwait0")
    def _():
        gram_from_behind(0)
    @stage("farpolar0")
    def _():
        rotation_into(gram_in.at[0], tour_ref[0, slot(-half - 1)], far_keep, far_move)
    @stage("early")
    def _():
        for k in range(len(PIECES)):
            early_move(k).wait()
        rotate_first(early_in, far_keep, early_kept, early)
        rotate_first(early_in, far_move, arrived, early)
        acc[...] = over_rows(kept[early, :], arrived[early, :])

    @stage("gram1")
    def _():

        head_move.wait_recv()
        acc[...] += over_rows(kept[head, :], arrived[head, :])

        @pl.loop(n_aside, n_chunks)
        def _(i):
            first_move(i).wait_recv()
            acc[...] += over_rows(kept[rows_of(i), :], arrived[rows_of(i), :])

    @stage("exch1")
    def _():
        side_move.start()
        summed_gram(1)
    @stage("polar1")
    def _():
        rotation_into(gram_out.at[1], tour_ref[1, slot(half)], keep_cols, move_cols)
    @stage("moves1")
    def _():

        @pl.loop(n_aside, n_chunks)
        def _(i):
            rotate_second(kept, arrived, move_cols, moved, low, rows_of(i))
            second_move(i).start()

        @pl.loop(0, height // TILE)
        def _(i):
            rotate_second(kept, arrived, keep_cols, out_ref, low, rows_of(i, TILE))

    @stage("gwait1")
    def _():
        gram_from_behind(1)
    @stage("farpolar1")
    def _():
        rotation_into(gram_in.at[1], tour_ref[1, slot(-1)], far_keep, far_move)
    @stage("side")
    def _():
        side_move.wait()
        late_move(0).wait()
        late_move(1).wait()
        rotate_second(early_kept, side_in, far_move, out_ref, high, aside)

    @stage("last")
    def _():

        head_move.wait_send()

        @pl.loop(n_aside, n_chunks)
        def _(i):
            first_move(i).wait_send()
            second_move(i).wait()


def shards(matrix, tournament):
    height, columns = matrix.shape
    width = columns // 2
    block = pltpu.VMEM((height, width), BF16)
    short = pltpu.VMEM((EARLY + LATE, width), BF16)
    cols = pltpu.VMEM((columns, width), BF16)
    grams = pltpu.VMEM((2, width, width), BF16)
    halves = pltpu.VMEM((2, width // 2, width), BF16)
    copies = pltpu.SemaphoreType.DMA((2, height // CHUNK))
    one = pltpu.SemaphoreType.DMA
    return pl.pallas_call(
        kernel,
        out_shape=pltpu.VMEM((height, columns), BF16),
        in_specs=[pl.BlockSpec(memory_space=pltpu.HBM), pl.BlockSpec(memory_space=pl.ANY)],
        out_specs=pl.BlockSpec(memory_space=pltpu.VMEM),
        scratch_shapes=[
            pltpu.SMEM(tournament.shape, jnp.int32), pltpu.SemaphoreType.DMA,
            pltpu.VMEM((height, columns), BF16), block, block, block, block,
            pltpu.VMEM((EARLY, columns), BF16), short, short, cols, cols, cols, cols,
            pltpu.VMEM((width, width), F32), pltpu.VMEM((2, width // 2, width), F32), halves, halves, grams, grams,
            pltpu.SemaphoreType.DMA((8,)), copies, copies,
            pltpu.SemaphoreType.DMA((10,)), pltpu.SemaphoreType.DMA((10,)),
            one((len(PIECES),)), one((len(PIECES),)), one((3,)), one((3,)),
        ],
        compiler_params=pltpu.CompilerParams(
            collective_id=0, has_side_effects=True, vmem_limit_bytes=56_000_000
        ),
    )(tournament, matrix)


def solution(mesh):
    placed = (P("samp", "pair"), P())
    return jax.shard_map(
        shards, mesh=mesh, in_specs=placed, out_specs=P("samp", "pair"), check_vma=False
    )
```

```python
import jax
import jax.numpy as jnp
from jax import lax
from jax.experimental import pallas as pl
from jax.experimental.pallas import tpu as pltpu
from jax.sharding import PartitionSpec as P

POLAR_STEPS = 5
MESH = pl.DeviceIdType.MESH
COUPLING = 2.0
START_SCALE = 6.0
CHUNK = 512
TILE = 512
EARLY = 256
LATE = 256
LATE_PIECES = ((0, 64), (64, 192))
PIECES = ((0, 128), (128, 128))
F32 = jnp.float32
BF16 = jnp.bfloat16


def over_rows(a, b):
    return lax.dot_general(a, b, (((0,), (0,)), ((), ())), preferred_element_type=F32)


def mul(a, b):
    return jnp.dot(a, b, preferred_element_type=F32)


def rotation_into(gram_ref, chosen, keep_ref, move_ref):
    gram = gram_ref[...].astype(F32)
    width = gram.shape[0]
    coupled = COUPLING * gram / jnp.sqrt(jnp.sum(gram * gram) + 1e-06)
    row = lax.broadcasted_iota(jnp.int32, (width, width), 0)
    eye = (row == lax.broadcasted_iota(jnp.int32, (width, width), 1)).astype(F32)
    halves = [jnp.concatenate([eye, -coupled], 1) / START_SCALE, jnp.concatenate([coupled.T, eye], 1) / START_SCALE]
    for _ in range(POLAR_STEPS):
        rounded = [h.astype(BF16) for h in halves]
        squares = [lax.dot_general(r, r, (((1,), (1,)), ((), ())), preferred_element_type=F32) for r in rounded]
        squares = [(-0.5 * q).astype(BF16) for q in squares]
        halves = [1.5 * h + mul(q, r) for h, q, r in zip(halves, squares, rounded)]
    last = chosen == 1
    for i, h in enumerate(halves):
        first_cols, second_cols = h[:, :width], h[:, width:]
        rows = pl.ds(i * width, width)
        keep_ref[rows, :] = jnp.where(last, second_cols, first_cols).astype(BF16)
        move_ref[rows, :] = jnp.where(last, first_cols, second_cols).astype(BF16)


def kernel(
    tour_hbm, y_hbm, out_ref,
    tour_ref, tour_sem,
    y_ref, kept, moving, arrived, moved, early_in, early_kept, side_in,
    keep_cols, move_cols, far_keep, far_move, acc, wide_in, narrow_out, narrow_in, gram_out, gram_in,
    load_sem, send_sem, recv_sem, ex_send, ex_recv, early_send, early_recv, side_send, side_recv,
):
    samp, pair = lax.axis_index("samp"), lax.axis_index("pair")
    slots = lax.axis_size("pair")
    half = slots // 2

    def slot(by):
        return lax.rem(pair + (by + slots), slots)

    ahead = {"pair": slot(half + 1)}
    side = {"pair": slot(2)}
    core_peer = {"samp": samp + 1 - 2 * lax.rem(samp, 2)}
    far_peer = {"samp": lax.rem(samp + 2, 4)}
    height, width = kept.shape
    low, high = pl.ds(0, width), pl.ds(width, width)
    early, aside = pl.ds(0, EARLY), pl.ds(0, EARLY + LATE)
    n_aside, n_chunks = (EARLY + LATE) // CHUNK, height // CHUNK
    head = pl.ds(EARLY, LATE)

    def rows_of(i, size=CHUNK):
        return pl.ds(pl.multiple_of(i * size, size), size)

    def stage(name):
        def run(body):
            with jax.named_scope(name):
                pl.when(samp >= 0)(body)

        return run

    def remote(source, target, send, recv, where):
        return pltpu.make_async_remote_copy(
            source, target, send, recv, device_id=where, device_id_type=MESH
        )

    n_loads = load_sem.shape[0]
    load_rows = height // n_loads
    loads = [
        pltpu.make_async_copy(y_hbm.at[pl.ds(i * load_rows, load_rows)], y_ref.at[pl.ds(i * load_rows, load_rows)], load_sem.at[i])
        for i in range(n_loads)
    ]
    for load in loads:
        load.start()
    tour_load = pltpu.make_async_copy(tour_hbm, tour_ref, tour_sem)
    tour_load.start()
    barrier = pltpu.get_barrier_semaphore()
    greeted = (ahead, {"pair": slot(-half - 1)}, side, {"pair": slot(-2)}, core_peer, far_peer)
    for where in greeted:
        pl.semaphore_signal(barrier, inc=1, device_id=where, device_id_type=MESH)

    core = lax.rem(samp, 2)
    part = width // 2
    my_part = pl.ds(pl.multiple_of(core * part, part), part)
    peer_part = pl.ds(pl.multiple_of((1 - core) * part, part), part)

    def exchange(source, target, step, kind, where):
        n = kind + 5 * step
        return remote(source, target, ex_send.at[n], ex_recv.at[n], where)

    def passed_gram(step):
        return exchange(gram_out.at[step, my_part], gram_in.at[step, my_part], step, 2, ahead)

    def summed_gram(step):
        near = exchange(acc.at[peer_part], wide_in.at[step], step, 0, core_peer)
        near.start()
        near.wait()
        chip = (acc[my_part, :] + wide_in[step]).astype(BF16)
        narrow_out[step] = chip
        far = exchange(narrow_out.at[step], narrow_in.at[step], step, 1, far_peer)
        far.start()
        far.wait()
        gram_out[step, my_part] = (chip.astype(F32) + narrow_in[step].astype(F32)).astype(BF16)
        share = exchange(gram_out.at[step, my_part], gram_out.at[step, my_part], step, 3, core_peer)
        share.start()
        if step == 0:
            early_move(1).start()
        else:
            late_move(1).start()
        passed_gram(step).start()
        share.wait()

    def gram_from_behind(step):
        passed_gram(step).wait()
        half_gram = gram_in.at[step, my_part]
        share = exchange(half_gram, half_gram, step, 4, core_peer)
        share.start()
        share.wait()

    def early_move(k):
        rows = pl.ds(*PIECES[k])
        return remote(y_hbm.at[rows], early_in.at[rows], early_send.at[k], early_recv.at[k], ahead)

    side_move = remote(moving.at[aside], side_in, side_send.at[0], side_recv.at[0], side)

    def late_move(k):
        start, count = LATE_PIECES[k]
        rows = pl.ds(EARLY + start, count)
        return remote(kept.at[rows], early_kept.at[rows], side_send.at[1 + k], side_recv.at[1 + k], ahead)

    def first_move(i, rows=None):
        rows = rows_of(i) if rows is None else rows
        return remote(moving.at[rows], arrived.at[rows], send_sem.at[0, i], recv_sem.at[0, i], ahead)

    head_move = first_move(0, head)

    def second_move(i):
        return remote(
            moved.at[rows_of(i)], out_ref.at[rows_of(i), high], send_sem.at[1, i], recv_sem.at[1, i], ahead
        )

    def rotate_first(from_ref, cols_ref, to_ref, rows):
        to_ref[rows, :] = mul(from_ref[rows, :], cols_ref[...]).astype(BF16)

    def rotate_second(kept_ref, moved_ref, cols_ref, to_ref, to_cols, rows):
        total = mul(kept_ref[rows, :], cols_ref[low, :]) + mul(moved_ref[rows, :], cols_ref[high, :])
        to_ref[rows, to_cols] = total.astype(BF16)

    with jax.named_scope("gram0"):
        acc[...] = jnp.zeros_like(acc)
        for i in range(n_loads):
            loads[i].wait()
            rows = pl.ds(i * load_rows, load_rows)
            acc[...] += over_rows(y_ref[rows, low], y_ref[rows, high])
            if i == 0:
                tour_load.wait()
                pl.semaphore_wait(barrier, len(greeted))
                early_move(0).start()

    @stage("exch0")
    def _():
        summed_gram(0)
    @stage("polar0")
    def _():
        rotation_into(gram_out.at[0], tour_ref[0, pair], keep_cols, move_cols)
    @stage("moves0")
    def _():

        rotate_first(y_ref, move_cols, moving, head)
        head_move.start()

        @pl.loop(n_aside, n_chunks)
        def _(i):
            rotate_first(y_ref, move_cols, moving, rows_of(i))
            first_move(i).start()

        rotate_first(y_ref, move_cols, moving, early)

        @pl.loop(0, height // TILE)
        def _(i):
            rotate_first(y_ref, keep_cols, kept, rows_of(i, TILE))

        late_move(0).start()

    @stage("gwait0")
    def _():
        gram_from_behind(0)
    @stage("farpolar0")
    def _():
        rotation_into(gram_in.at[0], tour_ref[0, slot(-half - 1)], far_keep, far_move)
    @stage("early")
    def _():
        for k in range(len(PIECES)):
            early_move(k).wait()
        rotate_first(early_in, far_keep, early_kept, early)
        rotate_first(early_in, far_move, arrived, early)
        acc[...] = over_rows(kept[early, :], arrived[early, :])

    @stage("gram1")
    def _():

        head_move.wait_recv()
        acc[...] += over_rows(kept[head, :], arrived[head, :])

        @pl.loop(n_aside, n_chunks)
        def _(i):
            first_move(i).wait_recv()
            acc[...] += over_rows(kept[rows_of(i), :], arrived[rows_of(i), :])

    @stage("exch1")
    def _():
        side_move.start()
        summed_gram(1)
    @stage("polar1")
    def _():
        rotation_into(gram_out.at[1], tour_ref[1, slot(half)], keep_cols, move_cols)
    @stage("moves1")
    def _():

        @pl.loop(n_aside, n_chunks)
        def _(i):
            rotate_second(kept, arrived, move_cols, moved, low, rows_of(i))
            second_move(i).start()

        @pl.loop(0, height // TILE)
        def _(i):
            rotate_second(kept, arrived, keep_cols, out_ref, low, rows_of(i, TILE))

    @stage("gwait1")
    def _():
        gram_from_behind(1)
    @stage("farpolar1")
    def _():
        rotation_into(gram_in.at[1], tour_ref[1, slot(-1)], far_keep, far_move)
    @stage("side")
    def _():
        side_move.wait()
        late_move(0).wait()
        late_move(1).wait()
        rotate_second(early_kept, side_in, far_move, out_ref, high, aside)

    @stage("last")
    def _():

        head_move.wait_send()

        @pl.loop(n_aside, n_chunks)
        def _(i):
            first_move(i).wait_send()
            second_move(i).wait()


def shards(matrix, tournament):
    height, columns = matrix.shape
    width = columns // 2
    block = pltpu.VMEM((height, width), BF16)
    short = pltpu.VMEM((EARLY + LATE, width), BF16)
    cols = pltpu.VMEM((columns, width), BF16)
    grams = pltpu.VMEM((2, width, width), BF16)
    halves = pltpu.VMEM((2, width // 2, width), BF16)
    copies = pltpu.SemaphoreType.DMA((2, height // CHUNK))
    one = pltpu.SemaphoreType.DMA
    return pl.pallas_call(
        kernel,
        out_shape=pltpu.VMEM((height, columns), BF16),
        in_specs=[pl.BlockSpec(memory_space=pltpu.HBM), pl.BlockSpec(memory_space=pl.ANY)],
        out_specs=pl.BlockSpec(memory_space=pltpu.VMEM),
        scratch_shapes=[
            pltpu.SMEM(tournament.shape, jnp.int32), pltpu.SemaphoreType.DMA,
            pltpu.VMEM((height, columns), BF16), block, block, block, block,
            pltpu.VMEM((EARLY, columns), BF16), short, short, cols, cols, cols, cols,
            pltpu.VMEM((width, width), F32), pltpu.VMEM((2, width // 2, width), F32), halves, halves, grams, grams,
            pltpu.SemaphoreType.DMA((4,)), copies, copies,
            pltpu.SemaphoreType.DMA((10,)), pltpu.SemaphoreType.DMA((10,)),
            one((len(PIECES),)), one((len(PIECES),)), one((3,)), one((3,)),
        ],
        compiler_params=pltpu.CompilerParams(
            collective_id=0, has_side_effects=True, vmem_limit_bytes=56_000_000
        ),
    )(tournament, matrix)


def solution(mesh):
    placed = (P("samp", "pair"), P())
    return jax.shard_map(
        shards, mesh=mesh, in_specs=placed, out_specs=P("samp", "pair"), check_vma=False
    )
```
